256 devices in a mesh: sx: 32 (over z_lo, x, y), sy: 8 (over z_hi, core).
Axes of the slice: x: 4, y: 4, z: 8 (z_hi: 4, z_lo: 2; z = z_hi * 2 + z_lo), core: 2. Of those that a mesh axis runs over, the one named last changes fastest.
Arguments:
- snapshots: bfloat16 [1024, 3, 64, 1024], P(None, None, 'sx', 'sy'), may hold values from -6 to 6
- quad_weight: float32 [3, 64, 1024], P(None, 'sx', 'sy'), may hold values from 0.5 to 1200
- mode_guess: float32 [16, 64, 2, 8], replicated, may hold values from -6 to 6
- bins: int32 [16], replicated, may hold values from 1 to 127
- starts: int32 [64], replicated, may hold values from 0 to 768
Outputs:
- modes: float32 [16, 2, 8, 3, 64, 1024], P(None, None, None, None, 'sx', 'sy')
- energy: float32 [16, 8], replicated
The draws below stay inside these ranges and needn't reach their ends.
All inputs are finite; a program needn't handle non-finite values.
Results may differ from the reference program's by a relative error of at most 0.0024.
Values may be sent and summed in bfloat16 or wider, within the bound.
No kernel may reach another device: no remote copies, remote signals or barrier semaphores. Data moves between devices by JAX's collectives and lax.ppermute only.
A program may use at most 64 MiB of HBM per device.

```python
import math
import jax
import jax.numpy as jnp
from jax import lax

NFFT = 256
NB = 64
NF = 16
NM = 8
TT = 1024
CX = 2
CY = 128
NSX = 64
NSY = 1024


def draw_quad_weight(key, part):
    key_base = jax.random.fold_in(key, 11)
    key_tile = jax.random.fold_in(key, 12)
    key_heavy = jax.random.fold_in(key, 13)
    base = jnp.exp(jax.random.uniform(key_base, (3, NSX, NSY), jnp.float32, math.log(0.5), math.log(4.0)))
    tiles_x = NSX // CX
    tiles_y = NSY // CY
    ntiles = tiles_x * tiles_y
    tile_factor = jnp.exp(jax.random.uniform(key_tile, (ntiles,), jnp.float32, 0.0, math.log(10.0)))
    heavy = jax.random.permutation(key_heavy, ntiles)[:2]
    tile_factor = tile_factor.at[heavy].set(300.0)
    row_tile = jnp.arange(NSX, dtype=jnp.int32) // CX
    col_tile = jnp.arange(NSY, dtype=jnp.int32) // CY
    tile_ids = row_tile[:, None] * tiles_y + col_tile[None, :]
    factor = tile_factor[tile_ids]
    return base * factor[None]


def set_ends(values, own_key, low, largest):
    longest = values.shape.index(max(values.shape))
    spots = []
    for shift in (0, 1):
        where = [jax.random.randint(jax.random.fold_in(own_key, axis), (), 0, length) for axis, length in enumerate(values.shape)]
        where[longest] = (where[longest] + shift) % values.shape[longest]
        spots.append(tuple(where))
    return values.at[spots[0]].set(low).at[spots[1]].set(largest)


def levels(own_key, extent, split, low, high):
    level = 1.0
    for dim, blocks in split:
        steps = jax.random.uniform(jax.random.fold_in(jax.random.fold_in(own_key, 6), dim), (blocks,), jnp.float32, low / len(split), high / len(split))
        level = level * jnp.repeat(jnp.exp(steps), extent[dim] // blocks).reshape((-1,) + (1,) * (len(extent) - 1 - dim))
    return level


def scatter_about(stream_key, shape, deviation, most, cuts=(), held_as=jnp.bfloat16):
    drawn = deviation * jax.random.normal(stream_key, shape, jnp.float32)
    if cuts:
        drawn = drawn * levels(stream_key, shape, cuts, -0.22, 0.18)
    return jnp.clip(drawn, -most, most).astype(held_as)


def setup_inputs(seed: int = 0) -> dict:
    keys = jax.random.split(jax.random.key(seed), 6)
    snapshots = scatter_about(keys[0], (TT, 3, NSX, NSY), 1.0, 6.0, ((2, 32), (3, 8)))
    quad_weight = draw_quad_weight(jax.random.fold_in(keys[5], 71), 0)
    mode_guess = scatter_about(keys[2], (NF, NB, 2, NM), 1.0, 6.0, (), jnp.float32)
    bins = set_ends(jax.random.randint(keys[3], (NF,), 1, NFFT // 2), jax.random.fold_in(keys[3], 1), 1, (NFFT // 2) - 1).astype(jnp.int32)
    starts = set_ends(jax.random.randint(keys[4], (NB,), 0, TT - NFFT + 1), jax.random.fold_in(keys[4], 1), 0, TT - NFFT).astype(jnp.int32)
    return {"snapshots": snapshots, "quad_weight": quad_weight, "mode_guess": mode_guess, "bins": bins, "starts": starts}


EPS = 1e-06

def make_twiddle(bins):
    steps = jnp.arange(NFFT, dtype=jnp.int32)
    window = 0.5 - 0.5 * jnp.cos(2.0 * jnp.pi * steps.astype(jnp.float32) / NFFT)
    norm_c = 1.0 / jnp.sqrt(jnp.sum(window * window))
    phase = bins[:, None] * steps[None, :] % NFFT
    angle = 2.0 * jnp.pi * phase.astype(jnp.float32) / NFFT
    twid = jnp.stack([norm_c * window * jnp.cos(angle), -(norm_c * window) * jnp.sin(angle)], axis=1)
    return twid.astype(jnp.bfloat16)

def weighted_slice(snapshots, quad_weight, twid, scale, starts, index):
    piece = lax.dynamic_index_in_dim(snapshots, index, 2, keepdims=False)
    times = starts[:, None] + jnp.arange(NFFT, dtype=jnp.int32)[None, :]
    windows = jnp.take(piece, times, axis=0)
    qhat = jnp.einsum('fpt,btvy->fpbvy', twid.astype(jnp.float32), windows.astype(jnp.float32))
    wslice = lax.dynamic_index_in_dim(quad_weight, index, 1, keepdims=False)
    colscale = scale[:, None] * jnp.sqrt(wslice)
    ydata = (qhat * colscale[None, None, None]).astype(jnp.bfloat16)
    return ydata.reshape(NF, 2 * NB, 3 * NSY)

def reference(snapshots, quad_weight, mode_guess, bins, starts):
    twid = make_twiddle(bins)

    def square_step(total, index):
        piece = lax.dynamic_index_in_dim(snapshots, index, 2, keepdims=False).astype(jnp.float32)
        wslice = lax.dynamic_index_in_dim(quad_weight, index, 1, keepdims=False)
        return (total + lax.optimization_barrier(jnp.sum(piece * piece * wslice[None], axis=(0, 2))), None)
    sums, _ = lax.scan(square_step, jnp.zeros((3,), jnp.float32), jnp.arange(NSX, dtype=jnp.int32))
    msq = sums / (TT * NSX * NSY)
    scale = lax.rsqrt(msq + EPS)

    def gram_step(total, index):
        ydata = weighted_slice(snapshots, quad_weight, twid, scale, starts, index).astype(jnp.float32)
        return (total + jnp.einsum('fax,fbx->fab', ydata, ydata), None)
    gram, _ = lax.scan(gram_step, jnp.zeros((NF, 2 * NB, 2 * NB), jnp.float32), jnp.arange(NSX, dtype=jnp.int32))
    gram_re = gram[:, :NB, :NB] + gram[:, NB:, NB:]
    gram_im = gram[:, :NB, NB:] - gram[:, NB:, :NB]
    denom = 3.0 * NSX * NSY
    gram_re = gram_re / denom
    gram_im = gram_im / denom
    hp = lax.Precision.HIGHEST
    guess_re = mode_guess[:, :, 0, :]
    guess_im = mode_guess[:, :, 1, :]
    zre = jnp.einsum('fbc,fcn->fbn', gram_re, guess_re, precision=hp) - jnp.einsum('fbc,fcn->fbn', gram_im, guess_im, precision=hp)
    zim = jnp.einsum('fbc,fcn->fbn', gram_re, guess_im, precision=hp) + jnp.einsum('fbc,fcn->fbn', gram_im, guess_re, precision=hp)
    norms = lax.optimization_barrier(jnp.sum(zre * zre + zim * zim, axis=1))
    energy = jnp.sqrt(norms / NB)
    inv = lax.rsqrt(norms + EPS)[:, None, :]
    coef_re = (zre * inv).astype(jnp.bfloat16)
    coef_im = (zim * inv).astype(jnp.bfloat16)
    upper = jnp.concatenate([coef_re, coef_im], axis=-1)
    lower = jnp.concatenate([-coef_im, coef_re], axis=-1)
    stacked = jnp.concatenate([upper, lower], axis=1).astype(jnp.float32)

    def mode_step(index):
        ydata = weighted_slice(snapshots, quad_weight, twid, scale, starts, index).astype(jnp.float32)
        return jnp.einsum('fan,fax->fnx', stacked, ydata).reshape(NF, 2, NM, 3, NSY)
    slices = lax.map(mode_step, jnp.arange(NSX, dtype=jnp.int32))
    modes = jnp.transpose(slices, (1, 2, 3, 4, 0, 5))
    return (modes, energy)
```

```python
import functools
import math

import jax
import jax.numpy as jnp
from jax import lax
from jax.experimental import pallas as pl
from jax.experimental.pallas import tpu as pltpu
from jax.sharding import Mesh
from jax.sharding import PartitionSpec as P

NFFT = 256
EPS = 1e-06
AXES = ("sx_0", "sx_1", "sx_2", "sy_0", "sy_1")
SX = AXES[:3]
SY = AXES[3:]
OWNERS = ("sx_1", "sx_2", "sy_1")
COLUMN = ("sx_0", "sy_0")
MIB = 1 << 20


def split3(x):
    hi = x.astype(jnp.bfloat16).astype(jnp.float32)
    mid = (x - hi).astype(jnp.bfloat16).astype(jnp.float32)
    lo = (x - hi - mid).astype(jnp.bfloat16).astype(jnp.float32)
    return hi, mid, lo


def split2(x):
    hi = x.astype(jnp.bfloat16)
    lo = (x - hi.astype(jnp.float32)).astype(jnp.bfloat16)
    return hi, lo


def local_kernel(starts_ref, bins_ref, x_ref, w_ref, g_ref, y_ref, pay_ref,
                 xf, xs, st, bn, ta, tb, win, amat, *, nf, nb, nt, nm, nv, nx):
    nvx = nv * nx
    half = nm // 2
    rows = nt * nvx
    chunk = rows // 8

    for i in range(8):
        xf[i * chunk:(i + 1) * chunk, :] = x_ref[i * chunk:(i + 1) * chunk, :].astype(jnp.float32)
    sums = []
    for v in range(nv):
        acc = jnp.zeros((1, 128), jnp.float32)
        for k in range(nx):
            col = v * nx + k
            part = xf[pl.ds(col, nt, stride=nvx), :]
            xs[:, col * 128:(col + 1) * 128] = part.astype(jnp.bfloat16)
            sq = jnp.sum(part * part, axis=0, keepdims=True)
            acc = acc + sq * w_ref[col:col + 1, :]
        sums.append(jnp.sum(acc, axis=1, keepdims=True))
    lane = lax.broadcasted_iota(jnp.int32, (1, 128), 1)
    msq_row = jnp.zeros((1, 128), jnp.float32)
    for v in range(nv):
        for k, piece in enumerate(split3(sums[v])):
            msq_row = jnp.where(lane == k * nv + v, piece, msq_row)
    tail = jnp.concatenate([msq_row, jnp.zeros((16 - nv * half - 1, 128), jnp.float32)], axis=0)

    for b in range(nb):
        st[b:b + 1, :] = jnp.full((1, 128), starts_ref[b], jnp.int32)
    for f in range(nf):
        bn[f:f + 1, :] = jnp.full((1, 128), bins_ref[f], jnp.int32)
    bn[nf:nf + 8, :] = jnp.ones((8, 128), jnp.int32)
    unit = 2.0 * math.pi / NFFT
    times = lax.broadcasted_iota(jnp.int32, (nf + 8, nt), 1)
    phase = ((bn[:, :1] * times) & (NFFT - 1)).astype(jnp.float32) * unit
    ta[0] = jnp.cos(phase)
    ta[1] = jnp.sin(phase)
    bin_lane = jnp.ones((1, 128), jnp.int32)
    for f in range(nf):
        bin_lane = jnp.where(lane == f, bins_ref[f], bin_lane)
    phase_b = ((st[:, :1] * bin_lane) & (NFFT - 1)).astype(jnp.float32) * unit
    tb[0] = jnp.cos(phase_b)
    tb[1] = jnp.sin(phase_b)
    norm_c = 1.0 / math.sqrt(sum((0.5 - 0.5 * math.cos(unit * t)) ** 2 for t in range(NFFT)))
    since = lax.broadcasted_iota(jnp.int32, (nb, nt), 1) - st[:, :1]
    cosd = ta[0, nf:nf + 1, :] * tb[0, :, nf:nf + 1] + ta[1, nf:nf + 1, :] * tb[1, :, nf:nf + 1]
    inside = (since >= 0) & (since < NFFT)
    win[...] = jnp.where(inside, norm_c * (0.5 - 0.5 * cosd), 0.0)

    low = lax.broadcasted_iota(jnp.int32, (nm, 2 * nb), 1) < nb
    sqrt_w = [jnp.sqrt(w_ref[c:c + 1, :]) for c in range(nvx)]
    sqrt_w = jnp.concatenate(sqrt_w, axis=1)
    for f in range(nf):
        slot = f % 2
        ca = ta[0, f:f + 1, :]
        sa = ta[1, f:f + 1, :]
        cb = tb[0, :, f:f + 1]
        sb = tb[1, :, f:f + 1]
        ww = win[...]
        amat[slot, :nb, :] = (ww * (ca * cb + sa * sb)).astype(jnp.bfloat16)
        amat[slot, nb:, :] = (ww * (ca * sb - sa * cb)).astype(jnp.bfloat16)
        q = jnp.dot(amat[slot], xs[...], preferred_element_type=jnp.float32)
        yf = (q * sqrt_w).astype(jnp.bfloat16)
        y_ref[f] = yf
        pr = g_ref[f, 0]
        pi = g_ref[f, 1]
        upper = jnp.concatenate([pr, -pi], axis=1)
        lower = jnp.concatenate([pi, pr], axis=1)
        guess = jnp.concatenate([upper, lower], axis=0)
        ghi, glo = split2(guess)
        proj = jnp.dot(jnp.concatenate([ghi, glo], axis=0), yf, preferred_element_type=jnp.float32)
        proj = proj[:2 * nm] + proj[2 * nm:]
        phi, plo = split2(proj)
        pst = jnp.concatenate([phi, plo], axis=0)
        zs = []
        span = nx * 128
        for v in range(nv):
            r = lax.dot_general(pst[:, v * span:(v + 1) * span], yf[:, v * span:(v + 1) * span],
                                (((1,), (1,)), ((), ())), preferred_element_type=jnp.float32)
            r = r[:2 * nm] + r[2 * nm:]
            ru = r[:nm]
            rv = pltpu.roll(r[nm:], nb, 1)
            zs.append(jnp.where(low, ru, -ru) + rv)
        for h in range(2):
            block = jnp.concatenate([z[h * half:(h + 1) * half] for z in zs] + [tail], axis=0)
            pay_ref[2 * f + h] = block.astype(jnp.bfloat16)


def partial_kernel(r_ref, o_ref):
    total = jnp.sum(r_ref[...].astype(jnp.float32), axis=0)
    for i in range(o_ref.shape[0]):
        o_ref[i] = total


def owner_kernel(r_ref, o_ref, s_ref, *, nv, half, count, denom):
    total = jnp.sum(r_ref[...], axis=0)
    row = total[nv * half:nv * half + 1, :]
    lane = lax.broadcasted_iota(jnp.int32, (1, 128), 1)
    z = jnp.zeros((half, 128), jnp.float32)
    for v in range(nv):
        mine = (lane == v) | (lane == nv + v) | (lane == 2 * nv + v)
        msq = jnp.sum(jnp.where(mine, row, 0.0), axis=1, keepdims=True) / count
        scale = lax.rsqrt(msq + EPS)
        s_ref[v:v + 1, :] = jnp.broadcast_to(scale, (1, 128))
        z = z + total[v * half:(v + 1) * half, :] * (scale * scale)
    s_ref[nv:, :] = jnp.zeros((8 - nv, 128), jnp.float32)
    z = z / denom
    norms = jnp.sum(z * z, axis=1, keepdims=True)
    coef = z * lax.rsqrt(norms + EPS)
    lanes = lax.broadcasted_iota(jnp.int32, (half, 128), 1)
    extra = jnp.zeros((half, 128), jnp.float32)
    for k, piece in enumerate(split3(norms)):
        extra = jnp.where(lanes == k, piece, extra)
    block = jnp.concatenate([coef, extra], axis=0).astype(jnp.bfloat16)
    for i in range(o_ref.shape[0]):
        o_ref[i] = block


def modes_kernel(c_ref, s_ref, y_ref, o_ref, e_ref, *, nf, nb, nm, nv, nx):
    half = nm // 2
    nvx = nv * nx
    low = lax.broadcasted_iota(jnp.int32, (nm, 2 * nb), 1) < nb
    lane = lax.broadcasted_iota(jnp.int32, (nm, nf), 1)
    energy = jnp.zeros((nm, nf), jnp.float32)
    for f in range(nf):
        both = c_ref[2 * f:2 * f + 2].astype(jnp.float32)
        coef = jnp.concatenate([both[0, :half], both[1, :half]], axis=0)
        extra = jnp.concatenate([both[0, half:], both[1, half:]], axis=0)
        norm = extra[:, 0:1] + extra[:, 1:2] + extra[:, 2:3]
        energy = jnp.where(lane == f, norm, energy)
        left = jnp.concatenate([jnp.where(low, coef, -coef), pltpu.roll(coef, nb, 1)], axis=0)
        m = jnp.dot(left.astype(jnp.bfloat16), y_ref[f], preferred_element_type=jnp.float32)
        base = f * 2 * nm * nvx
        for c in range(nvx):
            v = c // nx
            o_ref[pl.ds(base + c, 2 * nm, stride=nvx), :] = (
                m[:, c * 128:(c + 1) * 128] * s_ref[v:v + 1, :])
    e_ref[...] = jnp.sqrt(energy / nb)


def shards(snapshots, quad_weight, mode_guess, bins, starts):
    nt, nv, nx, ny = snapshots.shape
    nf, nb, _, nm = mode_guess.shape
    nvx = nv * nx
    half = nm // 2
    grid_points = nx * ny * lax.axis_size(SX) * lax.axis_size(SY)
    owners = lax.axis_size(OWNERS)
    column = lax.axis_size(COLUMN)
    vmem = pl.BlockSpec(memory_space=pltpu.VMEM)
    smem = pl.BlockSpec(memory_space=pltpu.SMEM)
    params = pltpu.CompilerParams(vmem_limit_bytes=40 * MIB)

    x = snapshots.reshape(nt * nvx, ny)
    w = quad_weight.reshape(nvx, ny)
    guess = jnp.transpose(mode_guess, (0, 2, 3, 1))
    y, payload = pl.pallas_call(
        functools.partial(local_kernel, nf=nf, nb=nb, nt=nt, nm=nm, nv=nv, nx=nx),
        out_shape=(jax.ShapeDtypeStruct((nf, 2 * nb, nvx * ny), jnp.bfloat16),
                   jax.ShapeDtypeStruct((2 * nf, 16, 128), jnp.bfloat16)),
        in_specs=[smem, smem, vmem, vmem, vmem],
        out_specs=(vmem, vmem),
        scratch_shapes=[
            pltpu.VMEM((nt * nvx, ny), jnp.float32),
            pltpu.VMEM((nt, nvx * ny), jnp.bfloat16),
            pltpu.VMEM((nb, 128), jnp.int32),
            pltpu.VMEM((nf + 8, 128), jnp.int32),
            pltpu.VMEM((2, nf + 8, nt), jnp.float32),
            pltpu.VMEM((2, nb, 128), jnp.float32),
            pltpu.VMEM((nb, nt), jnp.float32),
            pltpu.VMEM((2, 2 * nb, nt), jnp.bfloat16),
        ],
        compiler_params=params,
        name="local_part",
    )(starts, bins, x, w, guess)
    received = lax.all_to_all(payload, OWNERS, 0, 0, tiled=True)
    copies = pl.pallas_call(
        partial_kernel,
        out_shape=jax.ShapeDtypeStruct((column, 16, 128), jnp.float32),
        in_specs=[vmem], out_specs=vmem, compiler_params=params, name="plane_sum",
    )(received)
    received = lax.all_to_all(copies, COLUMN, 0, 0, tiled=True)
    copies, scale = pl.pallas_call(
        functools.partial(owner_kernel, nv=nv, half=half, count=float(nt * grid_points),
                          denom=float(nv * grid_points)),
        out_shape=(jax.ShapeDtypeStruct((owners, 2 * half, 128), jnp.bfloat16),
                   jax.ShapeDtypeStruct((8, 128), jnp.float32)),
        in_specs=[vmem], out_specs=(vmem, vmem), compiler_params=params, name="owner_part",
    )(received)
    coef = lax.all_to_all(copies, OWNERS, 0, 0, tiled=True)
    modes, energy = pl.pallas_call(
        functools.partial(modes_kernel, nf=nf, nb=nb, nm=nm, nv=nv, nx=nx),
        out_shape=(jax.ShapeDtypeStruct((nf * 2 * nm * nvx, ny), jnp.float32),
                   jax.ShapeDtypeStruct((nm, nf), jnp.float32)),
        in_specs=[vmem, vmem, vmem], out_specs=(vmem, vmem), compiler_params=params,
        name="modes_part",
    )(coef, scale, y)
    return modes.reshape(nf, 2, nm, nv, nx, ny), energy.T


def solution(mesh):
    finer = Mesh(mesh.devices.reshape(2, 4, 4, 4, 2), AXES)
    placed = (P(None, None, SX, SY), P(None, SX, SY), P(), P(), P())
    return jax.shard_map(
        shards,
        mesh=finer,
        in_specs=placed,
        out_specs=(P(None, None, None, None, SX, SY), P()),
        check_vma=False,
    )
```

```python
import functools
import math

import jax
import jax.numpy as jnp
from jax import lax
from jax.experimental import pallas as pl
from jax.experimental.pallas import tpu as pltpu
from jax.sharding import Mesh
from jax.sharding import PartitionSpec as P

NFFT = 256
EPS = 1e-06
AXES = ("sx_0", "sx_1", "sx_2", "sy_0", "sy_1")
SX = AXES[:3]
SY = AXES[3:]
OWNERS = ("sx_1", "sx_2", "sy_1")
COLUMN = ("sx_0", "sy_0")
MIB = 1 << 20


def split3(x):
    hi = x.astype(jnp.bfloat16).astype(jnp.float32)
    mid = (x - hi).astype(jnp.bfloat16).astype(jnp.float32)
    lo = (x - hi - mid).astype(jnp.bfloat16).astype(jnp.float32)
    return hi, mid, lo


def split2(x):
    hi = x.astype(jnp.bfloat16)
    lo = (x - hi.astype(jnp.float32)).astype(jnp.bfloat16)
    return hi, lo


def local_kernel(starts_hbm, bins_hbm, x_hbm, w_hbm, g_hbm, y_ref, pay_ref,
                 xb, xf, xs, wv, gv, st, bn, ta, tb, win, amat, starts_ref, bins_ref, sems,
                 *, nf, nb, nt, nm, nv, nx):
    nvx = nv * nx
    half = nm // 2
    rows = nt * nvx
    nchunk = xb.shape[0]
    chunk = rows // nchunk

    copies = [pltpu.make_async_copy(starts_hbm, starts_ref, sems.at[0]),
              pltpu.make_async_copy(bins_hbm, bins_ref, sems.at[1]),
              pltpu.make_async_copy(w_hbm, wv, sems.at[2]),
              pltpu.make_async_copy(g_hbm, gv, sems.at[3])]
    pieces = [pltpu.make_async_copy(x_hbm.at[pl.ds(i * chunk, chunk)], xb.at[i], sems.at[4 + i])
              for i in range(nchunk)]
    for c in copies[:2] + pieces + copies[2:]:
        c.start()
    copies[0].wait()
    copies[1].wait()

    lane = lax.broadcasted_iota(jnp.int32, (1, 128), 1)
    for b in range(nb):
        st[b:b + 1, :] = jnp.full((1, 128), starts_ref[b], jnp.int32)
    for f in range(nf):
        bn[f:f + 1, :] = jnp.full((1, 128), bins_ref[f], jnp.int32)
    bn[nf:nf + 8, :] = jnp.ones((8, 128), jnp.int32)
    unit = 2.0 * math.pi / NFFT
    times = lax.broadcasted_iota(jnp.int32, (nf + 8, nt), 1)
    phase = ((bn[:, :1] * times) & (NFFT - 1)).astype(jnp.float32) * unit
    ta[0] = jnp.cos(phase)
    ta[1] = jnp.sin(phase)
    bin_lane = jnp.ones((1, 128), jnp.int32)
    for f in range(nf):
        bin_lane = jnp.where(lane == f, bins_ref[f], bin_lane)
    phase_b = ((st[:, :1] * bin_lane) & (NFFT - 1)).astype(jnp.float32) * unit
    tb[0] = jnp.cos(phase_b)
    tb[1] = jnp.sin(phase_b)
    norm_c = 1.0 / math.sqrt(sum((0.5 - 0.5 * math.cos(unit * t)) ** 2 for t in range(NFFT)))
    since = lax.broadcasted_iota(jnp.int32, (nb, nt), 1) - st[:, :1]
    cosd = ta[0, nf:nf + 1, :] * tb[0, :, nf:nf + 1] + ta[1, nf:nf + 1, :] * tb[1, :, nf:nf + 1]
    inside = (since >= 0) & (since < NFFT)
    win[...] = jnp.where(inside, norm_c * (0.5 - 0.5 * cosd), 0.0)

    for i in range(nchunk):
        pieces[i].wait()
        xf[i * chunk:(i + 1) * chunk, :] = xb[i].astype(jnp.float32)
    copies[2].wait()
    copies[3].wait()
    sums = []
    for v in range(nv):
        acc = jnp.zeros((1, 128), jnp.float32)
        for k in range(nx):
            col = v * nx + k
            part = xf[pl.ds(col, nt, stride=nvx), :]
            xs[:, col * 128:(col + 1) * 128] = part.astype(jnp.bfloat16)
            sq = jnp.sum(part * part, axis=0, keepdims=True)
            acc = acc + sq * wv[v, k:k + 1, :]
        sums.append(jnp.sum(acc, axis=1, keepdims=True))
    msq_row = jnp.zeros((1, 128), jnp.float32)
    for v in range(nv):
        for k, piece in enumerate(split3(sums[v])):
            msq_row = jnp.where(lane == k * nv + v, piece, msq_row)
    tail = jnp.concatenate([msq_row, jnp.zeros((16 - nv * half - 1, 128), jnp.float32)], axis=0)

    low = lax.broadcasted_iota(jnp.int32, (nm, 2 * nb), 1) < nb
    sqrt_w = jnp.concatenate([jnp.sqrt(wv[c // nx, c % nx:c % nx + 1, :]) for c in range(nvx)], axis=1)
    span = nx * 128
    zeros = jnp.zeros((2 * nm, 2 * nb), jnp.float32)

    def transform(j):
        slot = j % 2
        for i in range(2):
            f = 2 * j + i
            ca = ta[0, f:f + 1, :]
            sa = ta[1, f:f + 1, :]
            cb = tb[0, :, f:f + 1]
            sb = tb[1, :, f:f + 1]
            ww = win[...]
            base = i * 2 * nb
            amat[slot, base:base + nb, :] = (ww * (ca * cb + sa * sb)).astype(jnp.bfloat16)
            amat[slot, base + nb:base + 2 * nb, :] = (ww * (ca * sb - sa * cb)).astype(jnp.bfloat16)
        q = jnp.dot(amat[slot], xs[...], preferred_element_type=jnp.float32)
        y_ref[4 * nb * j:4 * nb * (j + 1), :] = (q * sqrt_w).astype(jnp.bfloat16)

    def project(j):
        yf = y_ref[4 * nb * j:4 * nb * (j + 1), :]
        both = []
        for i in range(2):
            pr = gv[2 * j + i, 0]
            pi = gv[2 * j + i, 1]
            guess = jnp.concatenate([jnp.concatenate([pr, -pi], axis=1),
                                     jnp.concatenate([pi, pr], axis=1)], axis=0)
            both.append(jnp.concatenate([guess, zeros] if i == 0 else [zeros, guess], axis=1))
        ghi, glo = split2(jnp.concatenate(both, axis=0))
        proj = jnp.dot(jnp.concatenate([ghi, glo], axis=0), yf, preferred_element_type=jnp.float32)
        proj = proj[:4 * nm] + proj[4 * nm:]
        phi, plo = split2(proj)
        pst = jnp.concatenate([phi, plo], axis=0)
        zs = [[], []]
        for v in range(nv):
            r = lax.dot_general(pst[:, v * span:(v + 1) * span], yf[:, v * span:(v + 1) * span],
                                (((1,), (1,)), ((), ())), preferred_element_type=jnp.float32)
            r = r[:4 * nm] + r[4 * nm:]
            for i in range(2):
                part = r[i * 2 * nm:(i + 1) * 2 * nm, i * 2 * nb:(i + 1) * 2 * nb]
                ru = part[:nm]
                rv = pltpu.roll(part[nm:], nb, 1)
                zs[i].append(jnp.where(low, ru, -ru) + rv)
        for i in range(2):
            for h in range(2):
                block = jnp.concatenate([z[h * half:(h + 1) * half] for z in zs[i]] + [tail], axis=0)
                pay_ref[2 * (2 * j + i) + h] = block.astype(jnp.bfloat16)

    transform(0)
    for j in range(1, nf // 2):
        transform(j)
        project(j - 1)
    project(nf // 2 - 1)


def partial_kernel(r_ref, o_ref):
    total = jnp.sum(r_ref[...].astype(jnp.float32), axis=0)
    for i in range(o_ref.shape[0]):
        o_ref[i] = total


def owner_kernel(r_ref, o_ref, s_ref, *, nv, half, count, denom):
    total = jnp.sum(r_ref[...], axis=0)
    row = total[nv * half:nv * half + 1, :]
    lane = lax.broadcasted_iota(jnp.int32, (1, 128), 1)
    z = jnp.zeros((half, 128), jnp.float32)
    for v in range(nv):
        mine = (lane == v) | (lane == nv + v) | (lane == 2 * nv + v)
        msq = jnp.sum(jnp.where(mine, row, 0.0), axis=1, keepdims=True) / count
        scale = lax.rsqrt(msq + EPS)
        s_ref[v:v + 1, :] = jnp.broadcast_to(scale, (1, 128))
        z = z + total[v * half:(v + 1) * half, :] * (scale * scale)
    s_ref[nv:, :] = jnp.zeros((8 - nv, 128), jnp.float32)
    z = z / denom
    norms = jnp.sum(z * z, axis=1, keepdims=True)
    coef = z * lax.rsqrt(norms + EPS)
    lanes = lax.broadcasted_iota(jnp.int32, (half, 128), 1)
    extra = jnp.zeros((half, 128), jnp.float32)
    for k, piece in enumerate(split3(norms)):
        extra = jnp.where(lanes == k, piece, extra)
    block = jnp.concatenate([coef, extra], axis=0).astype(jnp.bfloat16)
    for i in range(o_ref.shape[0]):
        o_ref[i] = block


def modes_kernel(c_ref, s_ref, y_ref, o_ref, e_ref, *, nf, nb, nm, nv, nx):
    half = nm // 2
    nvx = nv * nx
    low = lax.broadcasted_iota(jnp.int32, (nm, 2 * nb), 1) < nb
    lane = lax.broadcasted_iota(jnp.int32, (nm, nf), 1)
    energy = jnp.zeros((nm, nf), jnp.float32)
    for f in range(nf):
        both = c_ref[2 * f:2 * f + 2].astype(jnp.float32)
        coef = jnp.concatenate([both[0, :half], both[1, :half]], axis=0)
        extra = jnp.concatenate([both[0, half:], both[1, half:]], axis=0)
        norm = extra[:, 0:1] + extra[:, 1:2] + extra[:, 2:3]
        energy = jnp.where(lane == f, norm, energy)
        left = jnp.concatenate([jnp.where(low, coef, -coef), pltpu.roll(coef, nb, 1)], axis=0)
        m = jnp.dot(left.astype(jnp.bfloat16), y_ref[2 * nb * f:2 * nb * (f + 1), :], preferred_element_type=jnp.float32)
        base = f * 2 * nm * nvx
        for c in range(nvx):
            v = c // nx
            o_ref[pl.ds(base + c, 2 * nm, stride=nvx), :] = (
                m[:, c * 128:(c + 1) * 128] * s_ref[v:v + 1, :])
    e_ref[...] = jnp.sqrt(energy / nb)


def shards(snapshots, quad_weight, mode_guess, bins, starts):
    nt, nv, nx, ny = snapshots.shape
    nf, nb, _, nm = mode_guess.shape
    nvx = nv * nx
    half = nm // 2
    grid_points = nx * ny * lax.axis_size(SX) * lax.axis_size(SY)
    owners = lax.axis_size(OWNERS)
    column = lax.axis_size(COLUMN)
    vmem = pl.BlockSpec(memory_space=pltpu.VMEM)
    hbm = pl.BlockSpec(memory_space=pltpu.HBM)
    params = pltpu.CompilerParams(vmem_limit_bytes=40 * MIB)

    x = snapshots.reshape(nt * nvx, ny)
    guess = jnp.transpose(mode_guess, (0, 2, 3, 1))
    nchunk = 4
    y, payload = pl.pallas_call(
        functools.partial(local_kernel, nf=nf, nb=nb, nt=nt, nm=nm, nv=nv, nx=nx),
        out_shape=(jax.ShapeDtypeStruct((nf * 2 * nb, nvx * ny), jnp.bfloat16),
                   jax.ShapeDtypeStruct((2 * nf, 16, 128), jnp.bfloat16)),
        in_specs=[hbm] * 5,
        out_specs=(vmem, vmem),
        scratch_shapes=[
            pltpu.VMEM((nchunk, nt * nvx // nchunk, ny), jnp.bfloat16),
            pltpu.VMEM((nt * nvx, ny), jnp.float32),
            pltpu.VMEM((nt, nvx * ny), jnp.bfloat16),
            pltpu.VMEM((nv, nx, ny), jnp.float32),
            pltpu.VMEM((nf, 2, nm, nb), jnp.float32),
            pltpu.VMEM((nb, 128), jnp.int32),
            pltpu.VMEM((nf + 8, 128), jnp.int32),
            pltpu.VMEM((2, nf + 8, nt), jnp.float32),
            pltpu.VMEM((2, nb, 128), jnp.float32),
            pltpu.VMEM((nb, nt), jnp.float32),
            pltpu.VMEM((2, 4 * nb, nt), jnp.bfloat16),
            pltpu.SMEM((nb,), jnp.int32),
            pltpu.SMEM((nf,), jnp.int32),
            pltpu.SemaphoreType.DMA((4 + nchunk,)),
        ],
        compiler_params=params,
        name="local_part",
    )(*[pltpu.with_memory_space_constraint(a, pltpu.HBM) for a in (starts, bins, x, quad_weight, guess)])
    received = lax.all_to_all(payload, OWNERS, 0, 0, tiled=True)
    copies = pl.pallas_call(
        partial_kernel,
        out_shape=jax.ShapeDtypeStruct((column, 16, 128), jnp.float32),
        in_specs=[vmem], out_specs=vmem, compiler_params=params, name="plane_sum",
    )(received)
    received = lax.all_to_all(copies, COLUMN, 0, 0, tiled=True)
    copies, scale = pl.pallas_call(
        functools.partial(owner_kernel, nv=nv, half=half, count=float(nt * grid_points),
                          denom=float(nv * grid_points)),
        out_shape=(jax.ShapeDtypeStruct((owners, 2 * half, 128), jnp.bfloat16),
                   jax.ShapeDtypeStruct((8, 128), jnp.float32)),
        in_specs=[vmem], out_specs=(vmem, vmem), compiler_params=params, name="owner_part",
    )(received)
    coef = lax.all_to_all(copies, OWNERS, 0, 0, tiled=True)
    modes, energy = pl.pallas_call(
        functools.partial(modes_kernel, nf=nf, nb=nb, nm=nm, nv=nv, nx=nx),
        out_shape=(jax.ShapeDtypeStruct((nf * 2 * nm * nvx, ny), jnp.float32),
                   jax.ShapeDtypeStruct((nm, nf), jnp.float32)),
        in_specs=[vmem, vmem, vmem], out_specs=(vmem, vmem), compiler_params=params,
        name="modes_part",
    )(coef, scale, y)
    return modes.reshape(nf, 2, nm, nv, nx, ny), energy.T


def solution(mesh):
    finer = Mesh(mesh.devices.reshape(2, 4, 4, 4, 2), AXES)
    placed = (P(None, None, SX, SY), P(None, SX, SY), P(), P(), P())
    return jax.shard_map(
        shards,
        mesh=finer,
        in_specs=placed,
        out_specs=(P(None, None, None, None, SX, SY), P()),
        check_vma=False,
    )
```

```python
import functools
import math

import jax
import jax.numpy as jnp
from jax import lax
from jax.experimental import pallas as pl
from jax.experimental.pallas import tpu as pltpu
from jax.sharding import Mesh
from jax.sharding import PartitionSpec as P

NFFT = 256
EPS = 1e-06
AXES = ("sx_0", "sx_1", "sx_2", "sy_0", "sy_1")
SX = AXES[:3]
SY = AXES[3:]
NEAR4 = ((0, 1), (1, 0), (2, 3), (3, 2))
RING4 = ((0, 3), (3, 0), (1, 2), (2, 1))
PAIR = ((0, 1), (1, 0))
STAGES = (("sx_0", PAIR), ("sx_1", NEAR4), ("sx_2", NEAR4), ("sx_1", RING4), ("sx_2", RING4),
          ("sy_0", NEAR4), ("sy_0", RING4))
CORE = "sy_1"
MIB = 1 << 20


def split3(x):
    hi = x.astype(jnp.bfloat16).astype(jnp.float32)
    mid = (x - hi).astype(jnp.bfloat16).astype(jnp.float32)
    lo = (x - hi - mid).astype(jnp.bfloat16).astype(jnp.float32)
    return hi, mid, lo


def split2(x):
    hi = x.astype(jnp.bfloat16)
    lo = (x - hi.astype(jnp.float32)).astype(jnp.bfloat16)
    return hi, lo


TAIL = 16


def as_rows(row):
    parts = split3(row)
    return jnp.concatenate(list(parts) + [jnp.zeros((TAIL - 3, 128), jnp.float32)], axis=0).astype(jnp.bfloat16)


def from_rows(tile):
    return tile[0:1] + tile[1:2] + tile[2:3]


def local_kernel(starts_hbm, bins_hbm, x_hbm, w_hbm, g_hbm, y_ref, mine_ref, other_ref,
                 xb, xf, xs, wv, gv, st, bn, ta, tb, win, amat, starts_ref, bins_ref, sems,
                 *, nf, nb, nt, nm, nv, nx):
    nvx = nv * nx
    rows = nt * nvx
    core = lax.axis_index(CORE)
    nchunk = xb.shape[0]
    chunk = rows // nchunk

    copies = [pltpu.make_async_copy(starts_hbm, starts_ref, sems.at[0]),
              pltpu.make_async_copy(bins_hbm, bins_ref, sems.at[1]),
              pltpu.make_async_copy(w_hbm, wv, sems.at[2]),
              pltpu.make_async_copy(g_hbm, gv, sems.at[3])]
    pieces = [pltpu.make_async_copy(x_hbm.at[pl.ds(i * chunk, chunk)], xb.at[i], sems.at[4 + i])
              for i in range(nchunk)]
    for c in copies[:2] + pieces + copies[2:]:
        c.start()
    copies[0].wait()
    copies[1].wait()

    lane = lax.broadcasted_iota(jnp.int32, (1, 128), 1)
    for b in range(nb):
        st[b:b + 1, :] = jnp.full((1, 128), starts_ref[b], jnp.int32)
    for f in range(nf):
        bn[f:f + 1, :] = jnp.full((1, 128), bins_ref[f], jnp.int32)
    bn[nf:nf + 8, :] = jnp.ones((8, 128), jnp.int32)
    unit = 2.0 * math.pi / NFFT
    times = lax.broadcasted_iota(jnp.int32, (nf + 8, nt), 1)
    phase = ((bn[:, :1] * times) & (NFFT - 1)).astype(jnp.float32) * unit
    ta[0] = jnp.cos(phase)
    ta[1] = jnp.sin(phase)
    bin_lane = jnp.ones((1, 128), jnp.int32)
    for f in range(nf):
        bin_lane = jnp.where(lane == f, bins_ref[f], bin_lane)
    phase_b = ((st[:, :1] * bin_lane) & (NFFT - 1)).astype(jnp.float32) * unit
    tb[0] = jnp.cos(phase_b)
    tb[1] = jnp.sin(phase_b)
    norm_c = 1.0 / math.sqrt(sum((0.5 - 0.5 * math.cos(unit * t)) ** 2 for t in range(NFFT)))
    since = lax.broadcasted_iota(jnp.int32, (nb, nt), 1) - st[:, :1]
    cosd = ta[0, nf:nf + 1, :] * tb[0, :, nf:nf + 1] + ta[1, nf:nf + 1, :] * tb[1, :, nf:nf + 1]
    inside = (since >= 0) & (since < NFFT)
    win[...] = jnp.where(inside, norm_c * (0.5 - 0.5 * cosd), 0.0)

    for i in range(nchunk):
        pieces[i].wait()
        xf[i * chunk:(i + 1) * chunk, :] = xb[i].astype(jnp.float32)
    copies[2].wait()
    copies[3].wait()
    sums = []
    for v in range(nv):
        acc = jnp.zeros((1, 128), jnp.float32)
        for k in range(nx):
            col = v * nx + k
            part = xf[pl.ds(col, nt, stride=nvx), :]
            xs[:, col * 128:(col + 1) * 128] = part.astype(jnp.bfloat16)
            sq = jnp.sum(part * part, axis=0, keepdims=True)
            acc = acc + sq * wv[v, k:k + 1, :]
        sums.append(jnp.sum(acc, axis=1, keepdims=True))
    msq = jnp.zeros((1, 128), jnp.float32)
    for v in range(nv):
        msq = jnp.where(lane == v, sums[v], msq)
    tail = as_rows(msq)
    mine_ref[mine_ref.shape[0] - TAIL:, :] = tail
    other_ref[other_ref.shape[0] - TAIL:, :] = tail

    low = lax.broadcasted_iota(jnp.int32, (nm, 2 * nb), 1) < nb
    sqrt_w = jnp.concatenate([jnp.sqrt(wv[c // nx, c % nx:c % nx + 1, :]) for c in range(nvx)], axis=1)
    span = nx * 128
    zeros = jnp.zeros((2 * nm, 2 * nb), jnp.float32)

    def transform(j):
        slot = j % 2
        for i in range(2):
            f = 2 * j + i
            ca = ta[0, f:f + 1, :]
            sa = ta[1, f:f + 1, :]
            cb = tb[0, :, f:f + 1]
            sb = tb[1, :, f:f + 1]
            ww = win[...]
            base = i * 2 * nb
            amat[slot, base:base + nb, :] = (ww * (ca * cb + sa * sb)).astype(jnp.bfloat16)
            amat[slot, base + nb:base + 2 * nb, :] = (ww * (ca * sb - sa * cb)).astype(jnp.bfloat16)
        q = jnp.dot(amat[slot], xs[...], preferred_element_type=jnp.float32)
        y_ref[4 * nb * j:4 * nb * (j + 1), :] = (q * sqrt_w).astype(jnp.bfloat16)

    def project(j):
        yf = y_ref[4 * nb * j:4 * nb * (j + 1), :]
        both = []
        for i in range(2):
            pr = gv[2 * j + i, 0]
            pi = gv[2 * j + i, 1]
            guess = jnp.concatenate([jnp.concatenate([pr, -pi], axis=1),
                                     jnp.concatenate([pi, pr], axis=1)], axis=0)
            both.append(jnp.concatenate([guess, zeros] if i == 0 else [zeros, guess], axis=1))
        ghi, glo = split2(jnp.concatenate(both, axis=0))
        proj = jnp.dot(jnp.concatenate([ghi, glo], axis=0), yf, preferred_element_type=jnp.float32)
        proj = proj[:4 * nm] + proj[4 * nm:]
        phi, plo = split2(proj)
        pst = jnp.concatenate([phi, plo], axis=0)
        zs = [[], []]
        for v in range(nv):
            r = lax.dot_general(pst[:, v * span:(v + 1) * span], yf[:, v * span:(v + 1) * span],
                                (((1,), (1,)), ((), ())), preferred_element_type=jnp.float32)
            r = r[:4 * nm] + r[4 * nm:]
            for i in range(2):
                part = r[i * 2 * nm:(i + 1) * 2 * nm, i * 2 * nb:(i + 1) * 2 * nb]
                ru = part[:nm]
                rv = pltpu.roll(part[nm:], nb, 1)
                zs[i].append(jnp.where(low, ru, -ru) + rv)
        npair = nf // 4
        base = (j % npair) * nv * 2 * nm

        def put(ref):
            for v in range(nv):
                block = jnp.concatenate([zs[0][v], zs[1][v]], axis=0).astype(jnp.bfloat16)
                ref[base + v * 2 * nm:base + (v + 1) * 2 * nm, :] = block

        pl.when(core == j // npair)(lambda: put(mine_ref))
        pl.when(core != j // npair)(lambda: put(other_ref))

    transform(0)
    for j in range(1, nf // 2):
        transform(j)
        project(j - 1)
    project(nf // 2 - 1)


def add_kernel(a_ref, b_ref, o_ref):
    cut = o_ref.shape[0] - TAIL
    total = a_ref[...].astype(jnp.float32) + b_ref[...].astype(jnp.float32)
    o_ref[:cut, :] = total[:cut].astype(jnp.bfloat16)
    o_ref[cut:, :] = as_rows(from_rows(total[cut:]))


def owner_kernel(a_ref, b_ref, o_ref, s_ref, *, nv, nm, count, denom):
    cut = a_ref.shape[0] - TAIL
    total = a_ref[...].astype(jnp.float32) + b_ref[...].astype(jnp.float32)
    msq = from_rows(total[cut:])
    scales = []
    for v in range(nv):
        scale = lax.rsqrt(jnp.broadcast_to(msq[:, v:v + 1], (1, 128)) / count + EPS)
        s_ref[v:v + 1, :] = scale
        scales.append(scale * scale)
    s_ref[nv:, :] = jnp.zeros((8 - nv, 128), jnp.float32)
    step = 2 * nm
    lanes = lax.broadcasted_iota(jnp.int32, (step, 128), 1)
    rows = cut // nv
    for j in range(rows // step):
        z = jnp.zeros((step, 128), jnp.float32)
        for v in range(nv):
            base = (j * nv + v) * step
            z = z + total[base:base + step] * scales[v]
        z = z / denom
        norms = jnp.sum(z * z, axis=1, keepdims=True)
        o_ref[j * step:(j + 1) * step, :] = (z * lax.rsqrt(norms + EPS)).astype(jnp.bfloat16)
        extra = jnp.zeros((step, 128), jnp.float32)
        for k, piece in enumerate(split3(norms)):
            extra = jnp.where(lanes == k, piece, extra)
        o_ref[rows + j * step:rows + (j + 1) * step, :] = extra.astype(jnp.bfloat16)


def modes_kernel(mine_ref, other_ref, s_ref, y_ref, o_ref, e_ref, *, nf, nb, nm, nv, nx):
    nvx = nv * nx
    core = lax.axis_index(CORE)
    first = core == 0
    mine = mine_ref[...].astype(jnp.float32)
    other = other_ref[...].astype(jnp.float32)
    halves = (jnp.where(first, mine, other), jnp.where(first, other, mine))
    rows = mine.shape[0] // 2
    low = lax.broadcasted_iota(jnp.int32, (nm, 2 * nb), 1) < nb
    lane = lax.broadcasted_iota(jnp.int32, (nm, nf), 1)
    energy = jnp.zeros((nm, nf), jnp.float32)
    for f in range(nf):
        part = halves[f // (nf // 2)]
        at = (f % (nf // 2)) * nm
        coef = part[at:at + nm]
        extra = part[rows + at:rows + at + nm]
        energy = jnp.where(lane == f, extra[:, 0:1] + extra[:, 1:2] + extra[:, 2:3], energy)
        left = jnp.concatenate([jnp.where(low, coef, -coef), pltpu.roll(coef, nb, 1)], axis=0)
        m = jnp.dot(left.astype(jnp.bfloat16), y_ref[2 * nb * f:2 * nb * (f + 1), :],
                    preferred_element_type=jnp.float32)
        base = f * 2 * nm * nvx
        for c in range(nvx):
            v = c // nx
            o_ref[pl.ds(base + c, 2 * nm, stride=nvx), :] = (
                m[:, c * 128:(c + 1) * 128] * s_ref[v:v + 1, :])
    e_ref[...] = jnp.sqrt(energy / nb)


def shards(snapshots, quad_weight, mode_guess, bins, starts):
    nt, nv, nx, ny = snapshots.shape
    nf, nb, _, nm = mode_guess.shape
    nvx = nv * nx
    grid_points = nx * ny * lax.axis_size(SX) * lax.axis_size(SY)
    vmem = pl.BlockSpec(memory_space=pltpu.VMEM)
    hbm = pl.BlockSpec(memory_space=pltpu.HBM)
    params = pltpu.CompilerParams(vmem_limit_bytes=40 * MIB)

    x = snapshots.reshape(nt * nvx, ny)
    guess = jnp.transpose(mode_guess, (0, 2, 3, 1))
    nchunk = 4
    packed = nf // 2 * nv * nm + TAIL
    y, mine, other = pl.pallas_call(
        functools.partial(local_kernel, nf=nf, nb=nb, nt=nt, nm=nm, nv=nv, nx=nx),
        out_shape=(jax.ShapeDtypeStruct((nf * 2 * nb, nvx * ny), jnp.bfloat16),
                   jax.ShapeDtypeStruct((packed, 128), jnp.bfloat16),
                   jax.ShapeDtypeStruct((packed, 128), jnp.bfloat16)),
        in_specs=[hbm] * 5,
        out_specs=(vmem, vmem, vmem),
        scratch_shapes=[
            pltpu.VMEM((nchunk, nt * nvx // nchunk, ny), jnp.bfloat16),
            pltpu.VMEM((nt * nvx, ny), jnp.float32),
            pltpu.VMEM((nt, nvx * ny), jnp.bfloat16),
            pltpu.VMEM((nv, nx, ny), jnp.float32),
            pltpu.VMEM((nf, 2, nm, nb), jnp.float32),
            pltpu.VMEM((nb, 128), jnp.int32),
            pltpu.VMEM((nf + 8, 128), jnp.int32),
            pltpu.VMEM((2, nf + 8, nt), jnp.float32),
            pltpu.VMEM((2, nb, 128), jnp.float32),
            pltpu.VMEM((nb, nt), jnp.float32),
            pltpu.VMEM((2, 4 * nb, nt), jnp.bfloat16),
            pltpu.SMEM((nb,), jnp.int32),
            pltpu.SMEM((nf,), jnp.int32),
            pltpu.SemaphoreType.DMA((4 + nchunk,)),
        ],
        compiler_params=params,
        name="local_part",
    )(*[pltpu.with_memory_space_constraint(a, pltpu.HBM) for a in (starts, bins, x, quad_weight, guess)])
    received = lax.ppermute(other, CORE, PAIR)
    for axis, pairs in STAGES:
        mine = pl.pallas_call(
            add_kernel,
            out_shape=jax.ShapeDtypeStruct((packed, 128), jnp.bfloat16),
            in_specs=[vmem, vmem], out_specs=vmem, compiler_params=params, name="add_partials",
        )(mine, received)
        received = lax.ppermute(mine, axis, pairs)
    coef, scale = pl.pallas_call(
        functools.partial(owner_kernel, nv=nv, nm=nm, count=float(nt * grid_points),
                          denom=float(nv * grid_points)),
        out_shape=(jax.ShapeDtypeStruct((nf * nm, 128), jnp.bfloat16),
                   jax.ShapeDtypeStruct((8, 128), jnp.float32)),
        in_specs=[vmem, vmem], out_specs=(vmem, vmem), compiler_params=params, name="owner_part",
    )(mine, received)
    coef_other = lax.ppermute(coef, CORE, PAIR)
    modes, energy = pl.pallas_call(
        functools.partial(modes_kernel, nf=nf, nb=nb, nm=nm, nv=nv, nx=nx),
        out_shape=(jax.ShapeDtypeStruct((nf * 2 * nm * nvx, ny), jnp.float32),
                   jax.ShapeDtypeStruct((nm, nf), jnp.float32)),
        in_specs=[vmem] * 4, out_specs=(vmem, vmem), compiler_params=params,
        name="modes_part",
    )(coef, coef_other, scale, y)
    return modes.reshape(nf, 2, nm, nv, nx, ny), energy.T


def solution(mesh):
    finer = Mesh(mesh.devices.reshape(2, 4, 4, 4, 2), AXES)
    placed = (P(None, None, SX, SY), P(None, SX, SY), P(), P(), P())
    return jax.shard_map(
        shards,
        mesh=finer,
        in_specs=placed,
        out_specs=(P(None, None, None, None, SX, SY), P()),
        check_vma=False,
    )
```

```python
import functools
import math

import jax
import jax.numpy as jnp
from jax import lax
from jax.experimental import pallas as pl
from jax.experimental.pallas import tpu as pltpu
from jax.sharding import Mesh
from jax.sharding import PartitionSpec as P

NFFT = 256
EPS = 1e-06
AXES = ("sx_0", "sx_1", "sx_2", "sy_0", "sy_1")
SX = AXES[:3]
SY = AXES[3:]
NEAR4 = ((0, 1), (1, 0), (2, 3), (3, 2))
RING4 = ((0, 3), (3, 0), (1, 2), (2, 1))
PAIR = ((0, 1), (1, 0))
STAGES = (("sx_0", PAIR), ("sx_1", NEAR4), ("sx_2", NEAR4), ("sx_1", RING4), ("sx_2", RING4),
          ("sy_0", NEAR4), ("sy_0", RING4))
CORE = "sy_1"
MIB = 1 << 20


def split3(x):
    hi = x.astype(jnp.bfloat16).astype(jnp.float32)
    mid = (x - hi).astype(jnp.bfloat16).astype(jnp.float32)
    lo = (x - hi - mid).astype(jnp.bfloat16).astype(jnp.float32)
    return hi, mid, lo


def split2(x):
    hi = x.astype(jnp.bfloat16)
    lo = (x - hi.astype(jnp.float32)).astype(jnp.bfloat16)
    return hi, lo


TAIL = 16


def as_rows(row):
    parts = split3(row)
    return jnp.concatenate(list(parts) + [jnp.zeros((TAIL - 3, 128), jnp.float32)], axis=0).astype(jnp.bfloat16)


def from_rows(tile):
    return tile[0:1] + tile[1:2] + tile[2:3]


def local_kernel(starts_hbm, bins_hbm, x_hbm, w_hbm, g_hbm, y_ref, mine_ref, other_ref,
                 xb, xf, xs, zall, wv, gv, st, bn, ta, tb, win, amat, starts_ref, bins_ref, sems,
                 *, nf, nb, nt, nm, nv, nx):
    nvx = nv * nx
    rows = nt * nvx
    core = lax.axis_index(CORE)
    nchunk = xb.shape[0]
    chunk = rows // nchunk

    copies = [pltpu.make_async_copy(starts_hbm, starts_ref, sems.at[0]),
              pltpu.make_async_copy(bins_hbm, bins_ref, sems.at[1]),
              pltpu.make_async_copy(w_hbm, wv, sems.at[2]),
              pltpu.make_async_copy(g_hbm, gv, sems.at[3])]
    pieces = [pltpu.make_async_copy(x_hbm.at[pl.ds(i * chunk, chunk)], xb.at[i], sems.at[4 + i])
              for i in range(nchunk)]
    for c in copies[:2] + pieces + copies[2:]:
        c.start()
    copies[0].wait()
    copies[1].wait()

    lane = lax.broadcasted_iota(jnp.int32, (1, 128), 1)
    for b in range(nb):
        st[b:b + 1, :] = jnp.full((1, 128), starts_ref[b], jnp.int32)
    for f in range(nf):
        bn[f:f + 1, :] = jnp.full((1, 128), bins_ref[f], jnp.int32)
    bn[nf:nf + 8, :] = jnp.ones((8, 128), jnp.int32)
    unit = 2.0 * math.pi / NFFT
    times = lax.broadcasted_iota(jnp.int32, (nf + 8, nt), 1)
    phase = ((bn[:, :1] * times) & (NFFT - 1)).astype(jnp.float32) * unit
    ta[0] = jnp.cos(phase)
    ta[1] = jnp.sin(phase)
    bin_lane = jnp.ones((1, 128), jnp.int32)
    for f in range(nf):
        bin_lane = jnp.where(lane == f, bins_ref[f], bin_lane)
    phase_b = ((st[:, :1] * bin_lane) & (NFFT - 1)).astype(jnp.float32) * unit
    tb[0] = jnp.cos(phase_b)
    tb[1] = jnp.sin(phase_b)
    norm_c = 1.0 / math.sqrt(sum((0.5 - 0.5 * math.cos(unit * t)) ** 2 for t in range(NFFT)))
    since = lax.broadcasted_iota(jnp.int32, (nb, nt), 1) - st[:, :1]
    cosd = ta[0, nf:nf + 1, :] * tb[0, :, nf:nf + 1] + ta[1, nf:nf + 1, :] * tb[1, :, nf:nf + 1]
    inside = (since >= 0) & (since < NFFT)
    win[...] = jnp.where(inside, norm_c * (0.5 - 0.5 * cosd), 0.0)

    for i in range(nchunk):
        pieces[i].wait()
        xf[i * chunk:(i + 1) * chunk, :] = xb[i].astype(jnp.float32)
    copies[2].wait()
    copies[3].wait()
    low = lax.broadcasted_iota(jnp.int32, (nm, 2 * nb), 1) < nb
    sqrt_w = jnp.concatenate([jnp.sqrt(wv[c // nx, c % nx:c % nx + 1, :]) for c in range(nvx)], axis=1)
    span = nx * 128
    zeros = jnp.zeros((2 * nm, 2 * nb), jnp.float32)

    def build(j):
        slot = j % 2
        for i in range(2):
            f = 2 * j + i
            ca = ta[0, f:f + 1, :]
            sa = ta[1, f:f + 1, :]
            cb = tb[0, :, f:f + 1]
            sb = tb[1, :, f:f + 1]
            ww = win[...]
            base = i * 2 * nb
            amat[slot, base:base + nb, :] = (ww * (ca * cb + sa * sb)).astype(jnp.bfloat16)
            amat[slot, base + nb:base + 2 * nb, :] = (ww * (ca * sb - sa * cb)).astype(jnp.bfloat16)

    def transform(j, v):
        cols = slice(v * span, (v + 1) * span)
        q = jnp.dot(amat[j % 2], xs[:, cols], preferred_element_type=jnp.float32)
        y_ref[4 * nb * j:4 * nb * (j + 1), cols] = (q * sqrt_w[:, cols]).astype(jnp.bfloat16)

    def project(j):
        yf = y_ref[4 * nb * j:4 * nb * (j + 1), :]
        both = []
        for i in range(2):
            pr = gv[2 * j + i, 0]
            pi = gv[2 * j + i, 1]
            guess = jnp.concatenate([jnp.concatenate([pr, -pi], axis=1),
                                     jnp.concatenate([pi, pr], axis=1)], axis=0)
            both.append(jnp.concatenate([guess, zeros] if i == 0 else [zeros, guess], axis=1))
        ghi, glo = split2(jnp.concatenate(both, axis=0))
        proj = jnp.dot(jnp.concatenate([ghi, glo], axis=0), yf, preferred_element_type=jnp.float32)
        proj = proj[:4 * nm] + proj[4 * nm:]
        phi, plo = split2(proj)
        pst = jnp.concatenate([phi, plo], axis=0)
        zs = [[], []]
        for v in range(nv):
            r = lax.dot_general(pst[:, v * span:(v + 1) * span], yf[:, v * span:(v + 1) * span],
                                (((1,), (1,)), ((), ())), preferred_element_type=jnp.float32)
            r = r[:4 * nm] + r[4 * nm:]
            for i in range(2):
                part = r[i * 2 * nm:(i + 1) * 2 * nm, i * 2 * nb:(i + 1) * 2 * nb]
                ru = part[:nm]
                rv = pltpu.roll(part[nm:], nb, 1)
                zs[i].append(jnp.where(low, ru, -ru) + rv)
        base = j * nv * 2 * nm
        for v in range(nv):
            block = jnp.concatenate([zs[0][v], zs[1][v]], axis=0).astype(jnp.bfloat16)
            zall[base + v * 2 * nm:base + (v + 1) * 2 * nm, :] = block

    build(0)
    sums = []
    for v in range(nv):
        acc = jnp.zeros((1, 128), jnp.float32)
        for k in range(nx):
            col = v * nx + k
            part = xf[pl.ds(col, nt, stride=nvx), :]
            xs[:, col * 128:(col + 1) * 128] = part.astype(jnp.bfloat16)
            sq = jnp.sum(part * part, axis=0, keepdims=True)
            acc = acc + sq * wv[v, k:k + 1, :]
        sums.append(jnp.sum(acc, axis=1, keepdims=True))
        transform(0, v)
    msq = jnp.zeros((1, 128), jnp.float32)
    for v in range(nv):
        msq = jnp.where(lane == v, sums[v], msq)
    tail = as_rows(msq)
    mine_ref[mine_ref.shape[0] - TAIL:, :] = tail
    other_ref[other_ref.shape[0] - TAIL:, :] = tail
    for j in range(1, nf // 2):
        build(j)
        for v in range(nv):
            transform(j, v)
        project(j - 1)
    project(nf // 2 - 1)
    cut = nf // 2 * nv * nm
    low_half = zall[:cut, :].astype(jnp.float32)
    high_half = zall[cut:, :].astype(jnp.float32)
    mine_ref[:cut, :] = jnp.where(core == 0, low_half, high_half).astype(jnp.bfloat16)
    other_ref[:cut, :] = jnp.where(core == 0, high_half, low_half).astype(jnp.bfloat16)


def add_kernel(a_ref, b_ref, o_ref):
    cut = o_ref.shape[0] - TAIL
    total = a_ref[...].astype(jnp.float32) + b_ref[...].astype(jnp.float32)
    o_ref[:cut, :] = total[:cut].astype(jnp.bfloat16)
    o_ref[cut:, :] = as_rows(from_rows(total[cut:]))


def owner_kernel(a_ref, b_ref, o_ref, s_ref, *, nv, nm, count, denom):
    cut = a_ref.shape[0] - TAIL
    total = a_ref[...].astype(jnp.float32) + b_ref[...].astype(jnp.float32)
    msq = from_rows(total[cut:])
    scales = []
    for v in range(nv):
        scale = lax.rsqrt(jnp.broadcast_to(msq[:, v:v + 1], (1, 128)) / count + EPS)
        s_ref[v:v + 1, :] = scale
        scales.append(scale * scale)
    s_ref[nv:, :] = jnp.zeros((8 - nv, 128), jnp.float32)
    step = 2 * nm
    lanes = lax.broadcasted_iota(jnp.int32, (step, 128), 1)
    rows = cut // nv
    for j in range(rows // step):
        z = jnp.zeros((step, 128), jnp.float32)
        for v in range(nv):
            base = (j * nv + v) * step
            z = z + total[base:base + step] * scales[v]
        z = z / denom
        norms = jnp.sum(z * z, axis=1, keepdims=True)
        o_ref[j * step:(j + 1) * step, :] = (z * lax.rsqrt(norms + EPS)).astype(jnp.bfloat16)
        extra = jnp.zeros((step, 128), jnp.float32)
        for k, piece in enumerate(split3(norms)):
            extra = jnp.where(lanes == k, piece, extra)
        o_ref[rows + j * step:rows + (j + 1) * step, :] = extra.astype(jnp.bfloat16)


def modes_kernel(mine_ref, other_ref, s_ref, y_ref, o_hbm, e_ref, ov, sems, *, nf, nb, nm, nv, nx):
    nvx = nv * nx
    core = lax.axis_index(CORE)
    first = core == 0
    mine = mine_ref[...].astype(jnp.float32)
    other = other_ref[...].astype(jnp.float32)
    halves = (jnp.where(first, mine, other), jnp.where(first, other, mine))
    rows = mine.shape[0] // 2
    low = lax.broadcasted_iota(jnp.int32, (nm, 2 * nb), 1) < nb
    lane = lax.broadcasted_iota(jnp.int32, (nm, nf), 1)
    energy = jnp.zeros((nm, nf), jnp.float32)
    zeros = jnp.zeros((2 * nm, 2 * nb), jnp.float32)
    pieces = sems.shape[0]
    per = ov.shape[0] // pieces
    outs = [pltpu.make_async_copy(ov.at[pl.ds(i * per, per)], o_hbm.at[pl.ds(i * per, per)], sems.at[i])
            for i in range(pieces)]
    pairs = nf // 2
    for j in range(pairs):
        left = []
        for i in range(2):
            f = 2 * j + i
            part = halves[f // (nf // 2)]
            at = (f % (nf // 2)) * nm
            coef = part[at:at + nm]
            extra = part[rows + at:rows + at + nm]
            energy = jnp.where(lane == f, extra[:, 0:1] + extra[:, 1:2] + extra[:, 2:3], energy)
            both = jnp.concatenate([jnp.where(low, coef, -coef), pltpu.roll(coef, nb, 1)], axis=0)
            left.append(jnp.concatenate([both, zeros] if i == 0 else [zeros, both], axis=1))
        left = jnp.concatenate(left, axis=0).astype(jnp.bfloat16)
        m = jnp.dot(left, y_ref[4 * nb * j:4 * nb * (j + 1), :], preferred_element_type=jnp.float32)
        base = j * 4 * nm * nvx
        for c in range(nvx):
            v = c // nx
            ov[pl.ds(base + c, 4 * nm, stride=nvx), :] = m[:, c * 128:(c + 1) * 128] * s_ref[v:v + 1, :]
        if (j + 1) % (pairs // pieces) == 0:
            outs[(j + 1) // (pairs // pieces) - 1].start()
    e_ref[...] = jnp.sqrt(energy / nb)
    for out in outs:
        out.wait()


def shards(snapshots, quad_weight, mode_guess, bins, starts):
    nt, nv, nx, ny = snapshots.shape
    nf, nb, _, nm = mode_guess.shape
    nvx = nv * nx
    grid_points = nx * ny * lax.axis_size(SX) * lax.axis_size(SY)
    vmem = pl.BlockSpec(memory_space=pltpu.VMEM)
    hbm = pl.BlockSpec(memory_space=pltpu.HBM)
    params = pltpu.CompilerParams(vmem_limit_bytes=40 * MIB)

    x = snapshots.reshape(nt * nvx, ny)
    guess = jnp.transpose(mode_guess, (0, 2, 3, 1))
    nchunk = 4
    packed = nf // 2 * nv * nm + TAIL
    y, mine, other = pl.pallas_call(
        functools.partial(local_kernel, nf=nf, nb=nb, nt=nt, nm=nm, nv=nv, nx=nx),
        out_shape=(jax.ShapeDtypeStruct((nf * 2 * nb, nvx * ny), jnp.bfloat16),
                   jax.ShapeDtypeStruct((packed, 128), jnp.bfloat16),
                   jax.ShapeDtypeStruct((packed, 128), jnp.bfloat16)),
        in_specs=[hbm] * 5,
        out_specs=(vmem, vmem, vmem),
        scratch_shapes=[
            pltpu.VMEM((nchunk, nt * nvx // nchunk, ny), jnp.bfloat16),
            pltpu.VMEM((nt * nvx, ny), jnp.float32),
            pltpu.VMEM((nt, nvx * ny), jnp.bfloat16),
            pltpu.VMEM((nf * nv * nm, 128), jnp.bfloat16),
            pltpu.VMEM((nv, nx, ny), jnp.float32),
            pltpu.VMEM((nf, 2, nm, nb), jnp.float32),
            pltpu.VMEM((nb, 128), jnp.int32),
            pltpu.VMEM((nf + 8, 128), jnp.int32),
            pltpu.VMEM((2, nf + 8, nt), jnp.float32),
            pltpu.VMEM((2, nb, 128), jnp.float32),
            pltpu.VMEM((nb, nt), jnp.float32),
            pltpu.VMEM((2, 4 * nb, nt), jnp.bfloat16),
            pltpu.SMEM((nb,), jnp.int32),
            pltpu.SMEM((nf,), jnp.int32),
            pltpu.SemaphoreType.DMA((4 + nchunk,)),
        ],
        compiler_params=params,
        name="local_part",
    )(*[pltpu.with_memory_space_constraint(a, pltpu.HBM) for a in (starts, bins, x, quad_weight, guess)])
    received = lax.ppermute(other, CORE, PAIR)
    for axis, pairs in STAGES:
        mine = pl.pallas_call(
            add_kernel,
            out_shape=jax.ShapeDtypeStruct((packed, 128), jnp.bfloat16),
            in_specs=[vmem, vmem], out_specs=vmem, compiler_params=params, name="add_partials",
        )(mine, received)
        received = lax.ppermute(mine, axis, pairs)
    coef, scale = pl.pallas_call(
        functools.partial(owner_kernel, nv=nv, nm=nm, count=float(nt * grid_points),
                          denom=float(nv * grid_points)),
        out_shape=(jax.ShapeDtypeStruct((nf * nm, 128), jnp.bfloat16),
                   jax.ShapeDtypeStruct((8, 128), jnp.float32)),
        in_specs=[vmem, vmem], out_specs=(vmem, vmem), compiler_params=params, name="owner_part",
    )(mine, received)
    coef_other = lax.ppermute(coef, CORE, PAIR)
    modes, energy = pl.pallas_call(
        functools.partial(modes_kernel, nf=nf, nb=nb, nm=nm, nv=nv, nx=nx),
        out_shape=(jax.ShapeDtypeStruct((nf * 2 * nm * nvx, ny), jnp.float32),
                   jax.ShapeDtypeStruct((nm, nf), jnp.float32)),
        in_specs=[vmem] * 4, out_specs=(hbm, vmem),
        scratch_shapes=[pltpu.VMEM((nf * 2 * nm * nvx, ny), jnp.float32), pltpu.SemaphoreType.DMA((4,))],
        compiler_params=params, name="modes_part",
    )(coef, coef_other, scale, y)
    return modes.reshape(nf, 2, nm, nv, nx, ny), energy.T


def solution(mesh):
    finer = Mesh(mesh.devices.reshape(2, 4, 4, 4, 2), AXES)
    placed = (P(None, None, SX, SY), P(None, SX, SY), P(), P(), P())
    return jax.shard_map(
        shards,
        mesh=finer,
        in_specs=placed,
        out_specs=(P(None, None, None, None, SX, SY), P()),
        check_vma=False,
    )
```

```python
import functools
import math

import jax
import jax.numpy as jnp
from jax import lax
from jax.experimental import pallas as pl
from jax.experimental.pallas import tpu as pltpu
from jax.sharding import Mesh
from jax.sharding import PartitionSpec as P
import numpy as np

NFFT = 256
EPS = 1e-06
AXES = ("sx_0", "sx_1", "sx_2", "sy_0", "sy_1")
SX = AXES[:3]
SY = AXES[3:]
SIZES = (2, 4, 4, 4, 2)
NEAR4 = (1, 0, 3, 2)
RING4 = (3, 2, 1, 0)
PAIR = (1, 0)
ORDER = (
    ((0, PAIR), (1, NEAR4), (2, NEAR4), (3, NEAR4), (1, RING4), (2, RING4), (3, RING4)),
    ((1, NEAR4), (0, PAIR), (3, NEAR4), (2, NEAR4), (3, RING4), (1, RING4), (2, RING4)),
)
CORE = "sy_1"
MIB = 1 << 20


def stage_pairs(stage):
    pairs = []
    for at in np.ndindex(*SIZES):
        axis, partner = ORDER[at[-1]][stage]
        to = list(at)
        to[axis] = partner[at[axis]]
        pairs.append((int(np.ravel_multi_index(at, SIZES)), int(np.ravel_multi_index(to, SIZES))))
    return pairs


def split3(x):
    hi = x.astype(jnp.bfloat16).astype(jnp.float32)
    mid = (x - hi).astype(jnp.bfloat16).astype(jnp.float32)
    lo = (x - hi - mid).astype(jnp.bfloat16).astype(jnp.float32)
    return hi, mid, lo


def split2(x):
    hi = x.astype(jnp.bfloat16)
    lo = (x - hi.astype(jnp.float32)).astype(jnp.bfloat16)
    return hi, lo


TAIL = 16


def as_rows(row):
    parts = split3(row)
    return jnp.concatenate(list(parts) + [jnp.zeros((TAIL - 3, 128), jnp.float32)], axis=0).astype(jnp.bfloat16)


def from_rows(tile):
    return tile[0:1] + tile[1:2] + tile[2:3]


def local_kernel(starts_hbm, bins_hbm, x_hbm, w_hbm, g_hbm, y_ref, mine_ref, other_ref,
                 xb, xf, xs, zall, wv, gv, st, bn, ta, tb, win, amat, starts_ref, bins_ref, sems,
                 *, nf, nb, nt, nm, nv, nx):
    nvx = nv * nx
    rows = nt * nvx
    core = lax.axis_index(CORE)
    nchunk = xb.shape[0]
    chunk = rows // nchunk

    copies = [pltpu.make_async_copy(starts_hbm, starts_ref, sems.at[0]),
              pltpu.make_async_copy(bins_hbm, bins_ref, sems.at[1]),
              pltpu.make_async_copy(w_hbm, wv, sems.at[2]),
              pltpu.make_async_copy(g_hbm, gv, sems.at[3])]
    pieces = [pltpu.make_async_copy(x_hbm.at[pl.ds(i * chunk, chunk)], xb.at[i], sems.at[4 + i])
              for i in range(nchunk)]
    for c in copies[:2] + pieces + copies[2:]:
        c.start()
    copies[0].wait()
    copies[1].wait()

    lane = lax.broadcasted_iota(jnp.int32, (1, 128), 1)
    for b in range(nb):
        st[b:b + 1, :] = jnp.full((1, 128), starts_ref[b], jnp.int32)
    for f in range(nf):
        bn[f:f + 1, :] = jnp.full((1, 128), bins_ref[f], jnp.int32)
    bn[nf:nf + 8, :] = jnp.ones((8, 128), jnp.int32)
    unit = 2.0 * math.pi / NFFT
    times = lax.broadcasted_iota(jnp.int32, (nf + 8, nt), 1)
    phase = ((bn[:, :1] * times) & (NFFT - 1)).astype(jnp.float32) * unit
    ta[0] = jnp.cos(phase)
    ta[1] = jnp.sin(phase)
    bin_lane = jnp.ones((1, 128), jnp.int32)
    for f in range(nf):
        bin_lane = jnp.where(lane == f, bins_ref[f], bin_lane)
    phase_b = ((st[:, :1] * bin_lane) & (NFFT - 1)).astype(jnp.float32) * unit
    tb[0] = jnp.cos(phase_b)
    tb[1] = jnp.sin(phase_b)
    norm_c = 1.0 / math.sqrt(sum((0.5 - 0.5 * math.cos(unit * t)) ** 2 for t in range(NFFT)))
    since = lax.broadcasted_iota(jnp.int32, (nb, nt), 1) - st[:, :1]
    cosd = ta[0, nf:nf + 1, :] * tb[0, :, nf:nf + 1] + ta[1, nf:nf + 1, :] * tb[1, :, nf:nf + 1]
    inside = (since >= 0) & (since < NFFT)
    win[...] = jnp.where(inside, norm_c * (0.5 - 0.5 * cosd), 0.0)

    for i in range(nchunk):
        pieces[i].wait()
        xf[i * chunk:(i + 1) * chunk, :] = xb[i].astype(jnp.float32)
    copies[2].wait()
    copies[3].wait()
    low = lax.broadcasted_iota(jnp.int32, (nm, 2 * nb), 1) < nb
    sqrt_w = jnp.concatenate([jnp.sqrt(wv[c // nx, c % nx:c % nx + 1, :]) for c in range(nvx)], axis=1)
    span = nx * 128
    zeros = jnp.zeros((2 * nm, 2 * nb), jnp.float32)

    def build(j):
        slot = j % 2
        for i in range(2):
            f = 2 * j + i
            ca = ta[0, f:f + 1, :]
            sa = ta[1, f:f + 1, :]
            cb = tb[0, :, f:f + 1]
            sb = tb[1, :, f:f + 1]
            ww = win[...]
            base = i * 2 * nb
            amat[slot, base:base + nb, :] = (ww * (ca * cb + sa * sb)).astype(jnp.bfloat16)
            amat[slot, base + nb:base + 2 * nb, :] = (ww * (ca * sb - sa * cb)).astype(jnp.bfloat16)

    def transform(j, v):
        cols = slice(v * span, (v + 1) * span)
        q = jnp.dot(amat[j % 2], xs[:, cols], preferred_element_type=jnp.float32)
        y_ref[4 * nb * j:4 * nb * (j + 1), cols] = (q * sqrt_w[:, cols]).astype(jnp.bfloat16)

    def project(j):
        yf = y_ref[4 * nb * j:4 * nb * (j + 1), :]
        both = []
        for i in range(2):
            pr = gv[2 * j + i, 0]
            pi = gv[2 * j + i, 1]
            guess = jnp.concatenate([jnp.concatenate([pr, -pi], axis=1),
                                     jnp.concatenate([pi, pr], axis=1)], axis=0)
            both.append(jnp.concatenate([guess, zeros] if i == 0 else [zeros, guess], axis=1))
        ghi, glo = split2(jnp.concatenate(both, axis=0))
        proj = jnp.dot(jnp.concatenate([ghi, glo], axis=0), yf, preferred_element_type=jnp.float32)
        proj = proj[:4 * nm] + proj[4 * nm:]
        phi, plo = split2(proj)
        pst = jnp.concatenate([phi, plo], axis=0)
        zs = [[], []]
        for v in range(nv):
            r = lax.dot_general(pst[:, v * span:(v + 1) * span], yf[:, v * span:(v + 1) * span],
                                (((1,), (1,)), ((), ())), preferred_element_type=jnp.float32)
            r = r[:4 * nm] + r[4 * nm:]
            for i in range(2):
                part = r[i * 2 * nm:(i + 1) * 2 * nm, i * 2 * nb:(i + 1) * 2 * nb]
                ru = part[:nm]
                rv = pltpu.roll(part[nm:], nb, 1)
                zs[i].append(jnp.where(low, ru, -ru) + rv)
        base = j * nv * 2 * nm
        for v in range(nv):
            block = jnp.concatenate([zs[0][v], zs[1][v]], axis=0).astype(jnp.bfloat16)
            zall[base + v * 2 * nm:base + (v + 1) * 2 * nm, :] = block

    build(0)
    sums = []
    for v in range(nv):
        acc = jnp.zeros((1, 128), jnp.float32)
        for k in range(nx):
            col = v * nx + k
            part = xf[pl.ds(col, nt, stride=nvx), :]
            xs[:, col * 128:(col + 1) * 128] = part.astype(jnp.bfloat16)
            sq = jnp.sum(part * part, axis=0, keepdims=True)
            acc = acc + sq * wv[v, k:k + 1, :]
        sums.append(jnp.sum(acc, axis=1, keepdims=True))
        transform(0, v)
    msq = jnp.zeros((1, 128), jnp.float32)
    for v in range(nv):
        msq = jnp.where(lane == v, sums[v], msq)
    tail = as_rows(msq)
    mine_ref[mine_ref.shape[0] - TAIL:, :] = tail
    other_ref[other_ref.shape[0] - TAIL:, :] = tail
    for j in range(1, nf // 2):
        build(j)
        for v in range(nv):
            transform(j, v)
        project(j - 1)
    project(nf // 2 - 1)
    cut = nf // 2 * nv * nm
    low_half = zall[:cut, :].astype(jnp.float32)
    high_half = zall[cut:, :].astype(jnp.float32)
    mine_ref[:cut, :] = jnp.where(core == 0, low_half, high_half).astype(jnp.bfloat16)
    other_ref[:cut, :] = jnp.where(core == 0, high_half, low_half).astype(jnp.bfloat16)


def add_kernel(a_ref, b_ref, o_ref):
    cut = o_ref.shape[0] - TAIL
    total = a_ref[...].astype(jnp.float32) + b_ref[...].astype(jnp.float32)
    o_ref[:cut, :] = total[:cut].astype(jnp.bfloat16)
    o_ref[cut:, :] = as_rows(from_rows(total[cut:]))


def owner_kernel(a_ref, b_ref, o_ref, s_ref, *, nv, nm, count, denom):
    cut = a_ref.shape[0] - TAIL
    total = a_ref[...].astype(jnp.float32) + b_ref[...].astype(jnp.float32)
    msq = from_rows(total[cut:])
    scales = []
    for v in range(nv):
        scale = lax.rsqrt(jnp.broadcast_to(msq[:, v:v + 1], (1, 128)) / count + EPS)
        s_ref[v:v + 1, :] = scale
        scales.append(scale * scale)
    s_ref[nv:, :] = jnp.zeros((8 - nv, 128), jnp.float32)
    step = 2 * nm
    lanes = lax.broadcasted_iota(jnp.int32, (step, 128), 1)
    rows = cut // nv
    for j in range(rows // step):
        z = jnp.zeros((step, 128), jnp.float32)
        for v in range(nv):
            base = (j * nv + v) * step
            z = z + total[base:base + step] * scales[v]
        z = z / denom
        norms = jnp.sum(z * z, axis=1, keepdims=True)
        o_ref[j * step:(j + 1) * step, :] = (z * lax.rsqrt(norms + EPS)).astype(jnp.bfloat16)
        extra = jnp.zeros((step, 128), jnp.float32)
        for k, piece in enumerate(split3(norms)):
            extra = jnp.where(lanes == k, piece, extra)
        o_ref[rows + j * step:rows + (j + 1) * step, :] = extra.astype(jnp.bfloat16)


def modes_kernel(mine_ref, other_ref, s_ref, y_ref, o_ref, e_ref, *, nf, nb, nm, nv, nx):
    nvx = nv * nx
    core = lax.axis_index(CORE)
    first = core == 0
    mine = mine_ref[...].astype(jnp.float32)
    other = other_ref[...].astype(jnp.float32)
    halves = (jnp.where(first, mine, other), jnp.where(first, other, mine))
    rows = mine.shape[0] // 2
    low = lax.broadcasted_iota(jnp.int32, (nm, 2 * nb), 1) < nb
    lane = lax.broadcasted_iota(jnp.int32, (nm, nf), 1)
    energy = jnp.zeros((nm, nf), jnp.float32)
    for f in range(nf):
        part = halves[f // (nf // 2)]
        at = (f % (nf // 2)) * nm
        coef = part[at:at + nm]
        extra = part[rows + at:rows + at + nm]
        energy = jnp.where(lane == f, extra[:, 0:1] + extra[:, 1:2] + extra[:, 2:3], energy)
        left = jnp.concatenate([jnp.where(low, coef, -coef), pltpu.roll(coef, nb, 1)], axis=0)
        m = jnp.dot(left.astype(jnp.bfloat16), y_ref[2 * nb * f:2 * nb * (f + 1), :],
                    preferred_element_type=jnp.float32)
        base = f * 2 * nm * nvx
        for c in range(nvx):
            v = c // nx
            o_ref[pl.ds(base + c, 2 * nm, stride=nvx), :] = (
                m[:, c * 128:(c + 1) * 128] * s_ref[v:v + 1, :])
    e_ref[...] = jnp.sqrt(energy / nb)


def shards(snapshots, quad_weight, mode_guess, bins, starts):
    nt, nv, nx, ny = snapshots.shape
    nf, nb, _, nm = mode_guess.shape
    nvx = nv * nx
    grid_points = nx * ny * lax.axis_size(SX) * lax.axis_size(SY)
    vmem = pl.BlockSpec(memory_space=pltpu.VMEM)
    hbm = pl.BlockSpec(memory_space=pltpu.HBM)
    params = pltpu.CompilerParams(vmem_limit_bytes=40 * MIB)

    x = snapshots.reshape(nt * nvx, ny)
    guess = jnp.transpose(mode_guess, (0, 2, 3, 1))
    nchunk = 4
    packed = nf // 2 * nv * nm + TAIL
    y, mine, other = pl.pallas_call(
        functools.partial(local_kernel, nf=nf, nb=nb, nt=nt, nm=nm, nv=nv, nx=nx),
        out_shape=(jax.ShapeDtypeStruct((nf * 2 * nb, nvx * ny), jnp.bfloat16),
                   jax.ShapeDtypeStruct((packed, 128), jnp.bfloat16),
                   jax.ShapeDtypeStruct((packed, 128), jnp.bfloat16)),
        in_specs=[hbm] * 5,
        out_specs=(vmem, vmem, vmem),
        scratch_shapes=[
            pltpu.VMEM((nchunk, nt * nvx // nchunk, ny), jnp.bfloat16),
            pltpu.VMEM((nt * nvx, ny), jnp.float32),
            pltpu.VMEM((nt, nvx * ny), jnp.bfloat16),
            pltpu.VMEM((nf * nv * nm, 128), jnp.bfloat16),
            pltpu.VMEM((nv, nx, ny), jnp.float32),
            pltpu.VMEM((nf, 2, nm, nb), jnp.float32),
            pltpu.VMEM((nb, 128), jnp.int32),
            pltpu.VMEM((nf + 8, 128), jnp.int32),
            pltpu.VMEM((2, nf + 8, nt), jnp.float32),
            pltpu.VMEM((2, nb, 128), jnp.float32),
            pltpu.VMEM((nb, nt), jnp.float32),
            pltpu.VMEM((2, 4 * nb, nt), jnp.bfloat16),
            pltpu.SMEM((nb,), jnp.int32),
            pltpu.SMEM((nf,), jnp.int32),
            pltpu.SemaphoreType.DMA((4 + nchunk,)),
        ],
        compiler_params=params,
        name="local_part",
    )(*[pltpu.with_memory_space_constraint(a, pltpu.HBM) for a in (starts, bins, x, quad_weight, guess)])
    swap = ((0, 1), (1, 0))
    received = lax.ppermute(other, CORE, swap)
    for stage in range(len(ORDER[0])):
        mine = pl.pallas_call(
            add_kernel,
            out_shape=jax.ShapeDtypeStruct((packed, 128), jnp.bfloat16),
            in_specs=[vmem, vmem], out_specs=vmem, compiler_params=params, name="add_partials",
        )(mine, received)
        received = lax.ppermute(mine, AXES, stage_pairs(stage))
    coef, scale = pl.pallas_call(
        functools.partial(owner_kernel, nv=nv, nm=nm, count=float(nt * grid_points),
                          denom=float(nv * grid_points)),
        out_shape=(jax.ShapeDtypeStruct((nf * nm, 128), jnp.bfloat16),
                   jax.ShapeDtypeStruct((8, 128), jnp.float32)),
        in_specs=[vmem, vmem], out_specs=(vmem, vmem), compiler_params=params, name="owner_part",
    )(mine, received)
    coef_other = lax.ppermute(coef, CORE, swap)
    modes, energy = pl.pallas_call(
        functools.partial(modes_kernel, nf=nf, nb=nb, nm=nm, nv=nv, nx=nx),
        out_shape=(jax.ShapeDtypeStruct((nf * 2 * nm * nvx, ny), jnp.float32),
                   jax.ShapeDtypeStruct((nm, nf), jnp.float32)),
        in_specs=[vmem] * 4, out_specs=(vmem, vmem), compiler_params=params,
        name="modes_part",
    )(coef, coef_other, scale, y)
    return modes.reshape(nf, 2, nm, nv, nx, ny), energy.T


def solution(mesh):
    finer = Mesh(mesh.devices.reshape(SIZES), AXES)
    placed = (P(None, None, SX, SY), P(None, SX, SY), P(), P(), P())
    return jax.shard_map(
        shards,
        mesh=finer,
        in_specs=placed,
        out_specs=(P(None, None, None, None, SX, SY), P()),
        check_vma=False,
    )
```

```python
import functools
import math

import jax
import jax.numpy as jnp
from jax import lax
from jax.experimental import pallas as pl
from jax.experimental.pallas import tpu as pltpu
from jax.sharding import Mesh
from jax.sharding import PartitionSpec as P
import numpy as np

NFFT = 256
EPS = 1e-06
AXES = ("sx_0", "sx_1", "sx_2", "sy_0", "sy_1")
SX = AXES[:3]
SY = AXES[3:]
SIZES = (2, 4, 4, 4, 2)
NEAR4 = (1, 0, 3, 2)
RING4 = (3, 2, 1, 0)
PAIR = (1, 0)
STAGES = ((0, PAIR), (1, NEAR4), (2, NEAR4), (1, RING4), (2, RING4), (3, NEAR4), (3, RING4))
CORE = "sy_1"
MIB = 1 << 20


def stage_pairs(axis, partner):
    pairs = []
    for at in np.ndindex(*SIZES):
        to = list(at)
        to[axis] = partner[at[axis]]
        to[-1] = 1 - at[-1]
        pairs.append((int(np.ravel_multi_index(at, SIZES)), int(np.ravel_multi_index(to, SIZES))))
    return pairs


def owned_half():
    total = lax.axis_index(AXES[0])
    for name in AXES[1:]:
        total = total + lax.axis_index(name)
    return total & 1


def split3(x):
    hi = x.astype(jnp.bfloat16).astype(jnp.float32)
    mid = (x - hi).astype(jnp.bfloat16).astype(jnp.float32)
    lo = (x - hi - mid).astype(jnp.bfloat16).astype(jnp.float32)
    return hi, mid, lo


def split2(x):
    hi = x.astype(jnp.bfloat16)
    lo = (x - hi.astype(jnp.float32)).astype(jnp.bfloat16)
    return hi, lo


TAIL = 16


def as_rows(row):
    parts = split3(row)
    return jnp.concatenate(list(parts) + [jnp.zeros((TAIL - 3, 128), jnp.float32)], axis=0).astype(jnp.bfloat16)


def from_rows(tile):
    return tile[0:1] + tile[1:2] + tile[2:3]


def local_kernel(starts_hbm, bins_hbm, x_hbm, w_hbm, g_hbm, y_ref, mine_ref, other_ref,
                 xb, xf, xs, zall, wv, gv, st, bn, ta, tb, win, amat, starts_ref, bins_ref, sems,
                 *, nf, nb, nt, nm, nv, nx):
    nvx = nv * nx
    rows = nt * nvx
    own = owned_half()
    nchunk = xb.shape[0]
    chunk = rows // nchunk

    copies = [pltpu.make_async_copy(starts_hbm, starts_ref, sems.at[0]),
              pltpu.make_async_copy(bins_hbm, bins_ref, sems.at[1]),
              pltpu.make_async_copy(w_hbm, wv, sems.at[2]),
              pltpu.make_async_copy(g_hbm, gv, sems.at[3])]
    pieces = [pltpu.make_async_copy(x_hbm.at[pl.ds(i * chunk, chunk)], xb.at[i], sems.at[4 + i])
              for i in range(nchunk)]
    for c in copies[:2] + pieces + copies[2:]:
        c.start()
    copies[0].wait()
    copies[1].wait()

    lane = lax.broadcasted_iota(jnp.int32, (1, 128), 1)
    for b in range(nb):
        st[b:b + 1, :] = jnp.full((1, 128), starts_ref[b], jnp.int32)
    for f in range(nf):
        bn[f:f + 1, :] = jnp.full((1, 128), bins_ref[f], jnp.int32)
    bn[nf:nf + 8, :] = jnp.ones((8, 128), jnp.int32)
    unit = 2.0 * math.pi / NFFT
    times = lax.broadcasted_iota(jnp.int32, (nf + 8, nt), 1)
    phase = ((bn[:, :1] * times) & (NFFT - 1)).astype(jnp.float32) * unit
    ta[0] = jnp.cos(phase)
    ta[1] = jnp.sin(phase)
    bin_lane = jnp.ones((1, 128), jnp.int32)
    for f in range(nf):
        bin_lane = jnp.where(lane == f, bins_ref[f], bin_lane)
    phase_b = ((st[:, :1] * bin_lane) & (NFFT - 1)).astype(jnp.float32) * unit
    tb[0] = jnp.cos(phase_b)
    tb[1] = jnp.sin(phase_b)
    norm_c = 1.0 / math.sqrt(sum((0.5 - 0.5 * math.cos(unit * t)) ** 2 for t in range(NFFT)))
    since = lax.broadcasted_iota(jnp.int32, (nb, nt), 1) - st[:, :1]
    cosd = ta[0, nf:nf + 1, :] * tb[0, :, nf:nf + 1] + ta[1, nf:nf + 1, :] * tb[1, :, nf:nf + 1]
    inside = (since >= 0) & (since < NFFT)
    win[...] = jnp.where(inside, norm_c * (0.5 - 0.5 * cosd), 0.0)

    for i in range(nchunk):
        pieces[i].wait()
        xf[i * chunk:(i + 1) * chunk, :] = xb[i].astype(jnp.float32)
    copies[2].wait()
    copies[3].wait()
    low = lax.broadcasted_iota(jnp.int32, (nm, 2 * nb), 1) < nb
    sqrt_w = jnp.concatenate([jnp.sqrt(wv[c // nx, c % nx:c % nx + 1, :]) for c in range(nvx)], axis=1)
    span = nx * 128
    zeros = jnp.zeros((2 * nm, 2 * nb), jnp.float32)

    def build(j):
        slot = j % 2
        for i in range(2):
            f = 2 * j + i
            ca = ta[0, f:f + 1, :]
            sa = ta[1, f:f + 1, :]
            cb = tb[0, :, f:f + 1]
            sb = tb[1, :, f:f + 1]
            ww = win[...]
            base = i * 2 * nb
            amat[slot, base:base + nb, :] = (ww * (ca * cb + sa * sb)).astype(jnp.bfloat16)
            amat[slot, base + nb:base + 2 * nb, :] = (ww * (ca * sb - sa * cb)).astype(jnp.bfloat16)

    def transform(j, v):
        cols = slice(v * span, (v + 1) * span)
        q = jnp.dot(amat[j % 2], xs[:, cols], preferred_element_type=jnp.float32)
        y_ref[4 * nb * j:4 * nb * (j + 1), cols] = (q * sqrt_w[:, cols]).astype(jnp.bfloat16)

    def project(j):
        yf = y_ref[4 * nb * j:4 * nb * (j + 1), :]
        both = []
        for i in range(2):
            pr = gv[2 * j + i, 0]
            pi = gv[2 * j + i, 1]
            guess = jnp.concatenate([jnp.concatenate([pr, -pi], axis=1),
                                     jnp.concatenate([pi, pr], axis=1)], axis=0)
            both.append(jnp.concatenate([guess, zeros] if i == 0 else [zeros, guess], axis=1))
        ghi, glo = split2(jnp.concatenate(both, axis=0))
        proj = jnp.dot(jnp.concatenate([ghi, glo], axis=0), yf, preferred_element_type=jnp.float32)
        proj = proj[:4 * nm] + proj[4 * nm:]
        phi, plo = split2(proj)
        pst = jnp.concatenate([phi, plo], axis=0)
        zs = [[], []]
        for v in range(nv):
            r = lax.dot_general(pst[:, v * span:(v + 1) * span], yf[:, v * span:(v + 1) * span],
                                (((1,), (1,)), ((), ())), preferred_element_type=jnp.float32)
            r = r[:4 * nm] + r[4 * nm:]
            for i in range(2):
                part = r[i * 2 * nm:(i + 1) * 2 * nm, i * 2 * nb:(i + 1) * 2 * nb]
                ru = part[:nm]
                rv = pltpu.roll(part[nm:], nb, 1)
                zs[i].append(jnp.where(low, ru, -ru) + rv)
        base = j * nv * 2 * nm
        for v in range(nv):
            block = jnp.concatenate([zs[0][v], zs[1][v]], axis=0).astype(jnp.bfloat16)
            zall[base + v * 2 * nm:base + (v + 1) * 2 * nm, :] = block

    build(0)
    sums = []
    for v in range(nv):
        acc = jnp.zeros((1, 128), jnp.float32)
        for k in range(nx):
            col = v * nx + k
            part = xf[pl.ds(col, nt, stride=nvx), :]
            xs[:, col * 128:(col + 1) * 128] = part.astype(jnp.bfloat16)
            sq = jnp.sum(part * part, axis=0, keepdims=True)
            acc = acc + sq * wv[v, k:k + 1, :]
        sums.append(jnp.sum(acc, axis=1, keepdims=True))
        transform(0, v)
    msq = jnp.zeros((1, 128), jnp.float32)
    for v in range(nv):
        msq = jnp.where(lane == v, sums[v], msq)
    tail = as_rows(msq)
    mine_ref[mine_ref.shape[0] - TAIL:, :] = tail
    other_ref[other_ref.shape[0] - TAIL:, :] = tail
    for j in range(1, nf // 2):
        build(j)
        for v in range(nv):
            transform(j, v)
        project(j - 1)
    project(nf // 2 - 1)
    cut = nf // 2 * nv * nm
    low_half = zall[:cut, :].astype(jnp.float32)
    high_half = zall[cut:, :].astype(jnp.float32)
    mine_ref[:cut, :] = jnp.where(own == 0, low_half, high_half).astype(jnp.bfloat16)
    other_ref[:cut, :] = jnp.where(own == 0, high_half, low_half).astype(jnp.bfloat16)


def add_kernel(a_ref, b_ref, o_ref):
    cut = o_ref.shape[0] - TAIL
    total = a_ref[...].astype(jnp.float32) + b_ref[...].astype(jnp.float32)
    o_ref[:cut, :] = total[:cut].astype(jnp.bfloat16)
    o_ref[cut:, :] = as_rows(from_rows(total[cut:]))


def owner_kernel(a_ref, b_ref, o_ref, s_ref, *, nv, nm, count, denom):
    cut = a_ref.shape[0] - TAIL
    total = a_ref[...].astype(jnp.float32) + b_ref[...].astype(jnp.float32)
    msq = from_rows(total[cut:])
    scales = []
    for v in range(nv):
        scale = lax.rsqrt(jnp.broadcast_to(msq[:, v:v + 1], (1, 128)) / count + EPS)
        s_ref[v:v + 1, :] = scale
        scales.append(scale * scale)
    s_ref[nv:, :] = jnp.zeros((8 - nv, 128), jnp.float32)
    step = 2 * nm
    lanes = lax.broadcasted_iota(jnp.int32, (step, 128), 1)
    rows = cut // nv
    for j in range(rows // step):
        z = jnp.zeros((step, 128), jnp.float32)
        for v in range(nv):
            base = (j * nv + v) * step
            z = z + total[base:base + step] * scales[v]
        z = z / denom
        norms = jnp.sum(z * z, axis=1, keepdims=True)
        o_ref[j * step:(j + 1) * step, :] = (z * lax.rsqrt(norms + EPS)).astype(jnp.bfloat16)
        extra = jnp.zeros((step, 128), jnp.float32)
        for k, piece in enumerate(split3(norms)):
            extra = jnp.where(lanes == k, piece, extra)
        o_ref[rows + j * step:rows + (j + 1) * step, :] = extra.astype(jnp.bfloat16)


def modes_kernel(mine_ref, other_ref, s_ref, y_ref, o_ref, e_ref, *, nf, nb, nm, nv, nx):
    nvx = nv * nx
    first = owned_half() == 0
    mine = mine_ref[...].astype(jnp.float32)
    other = other_ref[...].astype(jnp.float32)
    halves = (jnp.where(first, mine, other), jnp.where(first, other, mine))
    rows = mine.shape[0] // 2
    low = lax.broadcasted_iota(jnp.int32, (nm, 2 * nb), 1) < nb
    lane = lax.broadcasted_iota(jnp.int32, (nm, nf), 1)
    energy = jnp.zeros((nm, nf), jnp.float32)
    for f in range(nf):
        part = halves[f // (nf // 2)]
        at = (f % (nf // 2)) * nm
        coef = part[at:at + nm]
        extra = part[rows + at:rows + at + nm]
        energy = jnp.where(lane == f, extra[:, 0:1] + extra[:, 1:2] + extra[:, 2:3], energy)
        left = jnp.concatenate([jnp.where(low, coef, -coef), pltpu.roll(coef, nb, 1)], axis=0)
        m = jnp.dot(left.astype(jnp.bfloat16), y_ref[2 * nb * f:2 * nb * (f + 1), :],
                    preferred_element_type=jnp.float32)
        base = f * 2 * nm * nvx
        for c in range(nvx):
            v = c // nx
            o_ref[pl.ds(base + c, 2 * nm, stride=nvx), :] = (
                m[:, c * 128:(c + 1) * 128] * s_ref[v:v + 1, :])
    e_ref[...] = jnp.sqrt(energy / nb)


def shards(snapshots, quad_weight, mode_guess, bins, starts):
    nt, nv, nx, ny = snapshots.shape
    nf, nb, _, nm = mode_guess.shape
    nvx = nv * nx
    grid_points = nx * ny * lax.axis_size(SX) * lax.axis_size(SY)
    vmem = pl.BlockSpec(memory_space=pltpu.VMEM)
    hbm = pl.BlockSpec(memory_space=pltpu.HBM)
    params = pltpu.CompilerParams(vmem_limit_bytes=40 * MIB)

    x = snapshots.reshape(nt * nvx, ny)
    guess = jnp.transpose(mode_guess, (0, 2, 3, 1))
    nchunk = 4
    packed = nf // 2 * nv * nm + TAIL
    y, mine, other = pl.pallas_call(
        functools.partial(local_kernel, nf=nf, nb=nb, nt=nt, nm=nm, nv=nv, nx=nx),
        out_shape=(jax.ShapeDtypeStruct((nf * 2 * nb, nvx * ny), jnp.bfloat16),
                   jax.ShapeDtypeStruct((packed, 128), jnp.bfloat16),
                   jax.ShapeDtypeStruct((packed, 128), jnp.bfloat16)),
        in_specs=[hbm] * 5,
        out_specs=(vmem, vmem, vmem),
        scratch_shapes=[
            pltpu.VMEM((nchunk, nt * nvx // nchunk, ny), jnp.bfloat16),
            pltpu.VMEM((nt * nvx, ny), jnp.float32),
            pltpu.VMEM((nt, nvx * ny), jnp.bfloat16),
            pltpu.VMEM((nf * nv * nm, 128), jnp.bfloat16),
            pltpu.VMEM((nv, nx, ny), jnp.float32),
            pltpu.VMEM((nf, 2, nm, nb), jnp.float32),
            pltpu.VMEM((nb, 128), jnp.int32),
            pltpu.VMEM((nf + 8, 128), jnp.int32),
            pltpu.VMEM((2, nf + 8, nt), jnp.float32),
            pltpu.VMEM((2, nb, 128), jnp.float32),
            pltpu.VMEM((nb, nt), jnp.float32),
            pltpu.VMEM((2, 4 * nb, nt), jnp.bfloat16),
            pltpu.SMEM((nb,), jnp.int32),
            pltpu.SMEM((nf,), jnp.int32),
            pltpu.SemaphoreType.DMA((4 + nchunk,)),
        ],
        compiler_params=params,
        name="local_part",
    )(*[pltpu.with_memory_space_constraint(a, pltpu.HBM) for a in (starts, bins, x, quad_weight, guess)])
    swap = ((0, 1), (1, 0))
    received = lax.ppermute(other, CORE, swap)
    for stage in STAGES:
        mine = pl.pallas_call(
            add_kernel,
            out_shape=jax.ShapeDtypeStruct((packed, 128), jnp.bfloat16),
            in_specs=[vmem, vmem], out_specs=vmem, compiler_params=params, name="add_partials",
        )(mine, received)
        received = lax.ppermute(mine, AXES, stage_pairs(*stage))
    coef, scale = pl.pallas_call(
        functools.partial(owner_kernel, nv=nv, nm=nm, count=float(nt * grid_points),
                          denom=float(nv * grid_points)),
        out_shape=(jax.ShapeDtypeStruct((nf * nm, 128), jnp.bfloat16),
                   jax.ShapeDtypeStruct((8, 128), jnp.float32)),
        in_specs=[vmem, vmem], out_specs=(vmem, vmem), compiler_params=params, name="owner_part",
    )(mine, received)
    coef_other = lax.ppermute(coef, CORE, swap)
    modes, energy = pl.pallas_call(
        functools.partial(modes_kernel, nf=nf, nb=nb, nm=nm, nv=nv, nx=nx),
        out_shape=(jax.ShapeDtypeStruct((nf * 2 * nm * nvx, ny), jnp.float32),
                   jax.ShapeDtypeStruct((nm, nf), jnp.float32)),
        in_specs=[vmem] * 4, out_specs=(vmem, vmem), compiler_params=params,
        name="modes_part",
    )(coef, coef_other, scale, y)
    return modes.reshape(nf, 2, nm, nv, nx, ny), energy.T


def solution(mesh):
    finer = Mesh(mesh.devices.reshape(SIZES), AXES)
    placed = (P(None, None, SX, SY), P(None, SX, SY), P(), P(), P())
    return jax.shard_map(
        shards,
        mesh=finer,
        in_specs=placed,
        out_specs=(P(None, None, None, None, SX, SY), P()),
        check_vma=False,
    )
```

```python
import functools
import math

import jax
import jax.numpy as jnp
from jax import lax
from jax.experimental import pallas as pl
from jax.experimental.pallas import tpu as pltpu
from jax.sharding import Mesh
from jax.sharding import PartitionSpec as P
import numpy as np

NFFT = 256
EPS = 1e-06
AXES = ("sx_0", "sx_1", "sx_2", "sy_0", "sy_1")
SX = AXES[:3]
SY = AXES[3:]
SIZES = (2, 4, 4, 4, 2)
STEPS = (((0, 1), (3, 1)), ((1, 1), (1, 3)), ((2, 1), (2, 3)))
LAST = ((3, 3),)
CORE = "sy_1"
MIB = 1 << 20


def flip_pairs(*flips):
    pairs = []
    for at in np.ndindex(*SIZES):
        to = list(at)
        for axis, mask in flips:
            to[axis] ^= mask
            to[-1] ^= 1
        pairs.append((int(np.ravel_multi_index(at, SIZES)), int(np.ravel_multi_index(to, SIZES))))
    return pairs


def owned_half():
    total = lax.axis_index(AXES[0])
    for name in AXES[1:]:
        total = total + lax.axis_index(name)
    return total & 1


def split3(x):
    hi = x.astype(jnp.bfloat16).astype(jnp.float32)
    mid = (x - hi).astype(jnp.bfloat16).astype(jnp.float32)
    lo = (x - hi - mid).astype(jnp.bfloat16).astype(jnp.float32)
    return hi, mid, lo


def split2(x):
    hi = x.astype(jnp.bfloat16)
    lo = (x - hi.astype(jnp.float32)).astype(jnp.bfloat16)
    return hi, lo


TAIL = 16


def as_rows(row):
    parts = split3(row)
    return jnp.concatenate(list(parts) + [jnp.zeros((TAIL - 3, 128), jnp.float32)], axis=0).astype(jnp.bfloat16)


def from_rows(tile):
    return tile[0:1] + tile[1:2] + tile[2:3]


def local_kernel(starts_hbm, bins_hbm, x_hbm, w_hbm, g_hbm, y_ref, mine_ref, other_ref,
                 xb, xf, xs, zall, wv, gv, st, bn, ta, tb, win, amat, starts_ref, bins_ref, sems,
                 *, nf, nb, nt, nm, nv, nx):
    nvx = nv * nx
    rows = nt * nvx
    own = owned_half()
    nchunk = xb.shape[0]
    chunk = rows // nchunk

    copies = [pltpu.make_async_copy(starts_hbm, starts_ref, sems.at[0]),
              pltpu.make_async_copy(bins_hbm, bins_ref, sems.at[1]),
              pltpu.make_async_copy(w_hbm, wv, sems.at[2]),
              pltpu.make_async_copy(g_hbm, gv, sems.at[3])]
    pieces = [pltpu.make_async_copy(x_hbm.at[pl.ds(i * chunk, chunk)], xb.at[i], sems.at[4 + i])
              for i in range(nchunk)]
    for c in copies[:2] + pieces + copies[2:]:
        c.start()
    copies[0].wait()
    copies[1].wait()

    lane = lax.broadcasted_iota(jnp.int32, (1, 128), 1)
    for b in range(nb):
        st[b:b + 1, :] = jnp.full((1, 128), starts_ref[b], jnp.int32)
    for f in range(nf):
        bn[f:f + 1, :] = jnp.full((1, 128), bins_ref[f], jnp.int32)
    bn[nf:nf + 8, :] = jnp.ones((8, 128), jnp.int32)
    unit = 2.0 * math.pi / NFFT
    times = lax.broadcasted_iota(jnp.int32, (nf + 8, nt), 1)
    phase = ((bn[:, :1] * times) & (NFFT - 1)).astype(jnp.float32) * unit
    ta[0] = jnp.cos(phase)
    ta[1] = jnp.sin(phase)
    bin_lane = jnp.ones((1, 128), jnp.int32)
    for f in range(nf):
        bin_lane = jnp.where(lane == f, bins_ref[f], bin_lane)
    phase_b = ((st[:, :1] * bin_lane) & (NFFT - 1)).astype(jnp.float32) * unit
    tb[0] = jnp.cos(phase_b)
    tb[1] = jnp.sin(phase_b)
    norm_c = 1.0 / math.sqrt(sum((0.5 - 0.5 * math.cos(unit * t)) ** 2 for t in range(NFFT)))
    since = lax.broadcasted_iota(jnp.int32, (nb, nt), 1) - st[:, :1]
    cosd = ta[0, nf:nf + 1, :] * tb[0, :, nf:nf + 1] + ta[1, nf:nf + 1, :] * tb[1, :, nf:nf + 1]
    inside = (since >= 0) & (since < NFFT)
    win[...] = jnp.where(inside, norm_c * (0.5 - 0.5 * cosd), 0.0)

    for i in range(nchunk):
        pieces[i].wait()
        xf[i * chunk:(i + 1) * chunk, :] = xb[i].astype(jnp.float32)
    copies[2].wait()
    copies[3].wait()
    low = lax.broadcasted_iota(jnp.int32, (nm, 2 * nb), 1) < nb
    sqrt_w = jnp.concatenate([jnp.sqrt(wv[c // nx, c % nx:c % nx + 1, :]) for c in range(nvx)], axis=1)
    span = nx * 128
    zeros = jnp.zeros((2 * nm, 2 * nb), jnp.float32)

    def build(j):
        slot = j % 2
        for i in range(2):
            f = 2 * j + i
            ca = ta[0, f:f + 1, :]
            sa = ta[1, f:f + 1, :]
            cb = tb[0, :, f:f + 1]
            sb = tb[1, :, f:f + 1]
            ww = win[...]
            base = i * 2 * nb
            amat[slot, base:base + nb, :] = (ww * (ca * cb + sa * sb)).astype(jnp.bfloat16)
            amat[slot, base + nb:base + 2 * nb, :] = (ww * (ca * sb - sa * cb)).astype(jnp.bfloat16)

    def transform(j, v):
        cols = slice(v * span, (v + 1) * span)
        q = jnp.dot(amat[j % 2], xs[:, cols], preferred_element_type=jnp.float32)
        y_ref[4 * nb * j:4 * nb * (j + 1), cols] = (q * sqrt_w[:, cols]).astype(jnp.bfloat16)

    def project(j):
        yf = y_ref[4 * nb * j:4 * nb * (j + 1), :]
        both = []
        for i in range(2):
            pr = gv[2 * j + i, 0]
            pi = gv[2 * j + i, 1]
            guess = jnp.concatenate([jnp.concatenate([pr, -pi], axis=1),
                                     jnp.concatenate([pi, pr], axis=1)], axis=0)
            both.append(jnp.concatenate([guess, zeros] if i == 0 else [zeros, guess], axis=1))
        ghi, glo = split2(jnp.concatenate(both, axis=0))
        proj = jnp.dot(jnp.concatenate([ghi, glo], axis=0), yf, preferred_element_type=jnp.float32)
        proj = proj[:4 * nm] + proj[4 * nm:]
        phi, plo = split2(proj)
        pst = jnp.concatenate([phi, plo], axis=0)
        zs = [[], []]
        for v in range(nv):
            r = lax.dot_general(pst[:, v * span:(v + 1) * span], yf[:, v * span:(v + 1) * span],
                                (((1,), (1,)), ((), ())), preferred_element_type=jnp.float32)
            r = r[:4 * nm] + r[4 * nm:]
            for i in range(2):
                part = r[i * 2 * nm:(i + 1) * 2 * nm, i * 2 * nb:(i + 1) * 2 * nb]
                ru = part[:nm]
                rv = pltpu.roll(part[nm:], nb, 1)
                zs[i].append(jnp.where(low, ru, -ru) + rv)
        base = j * nv * 2 * nm
        for v in range(nv):
            block = jnp.concatenate([zs[0][v], zs[1][v]], axis=0).astype(jnp.bfloat16)
            zall[base + v * 2 * nm:base + (v + 1) * 2 * nm, :] = block

    build(0)
    sums = []
    for v in range(nv):
        acc = jnp.zeros((1, 128), jnp.float32)
        for k in range(nx):
            col = v * nx + k
            part = xf[pl.ds(col, nt, stride=nvx), :]
            xs[:, col * 128:(col + 1) * 128] = part.astype(jnp.bfloat16)
            sq = jnp.sum(part * part, axis=0, keepdims=True)
            acc = acc + sq * wv[v, k:k + 1, :]
        sums.append(jnp.sum(acc, axis=1, keepdims=True))
        transform(0, v)
    msq = jnp.zeros((1, 128), jnp.float32)
    for v in range(nv):
        msq = jnp.where(lane == v, sums[v], msq)
    tail = as_rows(msq)
    mine_ref[mine_ref.shape[0] - TAIL:, :] = tail
    other_ref[other_ref.shape[0] - TAIL:, :] = tail
    for j in range(1, nf // 2):
        build(j)
        for v in range(nv):
            transform(j, v)
        project(j - 1)
    project(nf // 2 - 1)
    cut = nf // 2 * nv * nm
    low_half = zall[:cut, :].astype(jnp.float32)
    high_half = zall[cut:, :].astype(jnp.float32)
    mine_ref[:cut, :] = jnp.where(own == 0, low_half, high_half).astype(jnp.bfloat16)
    other_ref[:cut, :] = jnp.where(own == 0, high_half, low_half).astype(jnp.bfloat16)


def add_kernel(*refs):
    o_ref = refs[-1]
    cut = o_ref.shape[0] - TAIL
    terms = [r[...].astype(jnp.float32) for r in refs[:-1]]
    while len(terms) > 1:
        terms = [terms[i] + terms[i + 1] for i in range(0, len(terms), 2)]
    total = terms[0]
    o_ref[:cut, :] = total[:cut].astype(jnp.bfloat16)
    o_ref[cut:, :] = as_rows(from_rows(total[cut:]))


def owner_kernel(a_ref, b_ref, o_ref, s_ref, *, nv, nm, count, denom):
    cut = a_ref.shape[0] - TAIL
    total = a_ref[...].astype(jnp.float32) + b_ref[...].astype(jnp.float32)
    msq = from_rows(total[cut:])
    scales = []
    for v in range(nv):
        scale = lax.rsqrt(jnp.broadcast_to(msq[:, v:v + 1], (1, 128)) / count + EPS)
        s_ref[v:v + 1, :] = scale
        scales.append(scale * scale)
    s_ref[nv:, :] = jnp.zeros((8 - nv, 128), jnp.float32)
    step = 2 * nm
    lanes = lax.broadcasted_iota(jnp.int32, (step, 128), 1)
    rows = cut // nv
    for j in range(rows // step):
        z = jnp.zeros((step, 128), jnp.float32)
        for v in range(nv):
            base = (j * nv + v) * step
            z = z + total[base:base + step] * scales[v]
        z = z / denom
        norms = jnp.sum(z * z, axis=1, keepdims=True)
        o_ref[j * step:(j + 1) * step, :] = (z * lax.rsqrt(norms + EPS)).astype(jnp.bfloat16)
        extra = jnp.zeros((step, 128), jnp.float32)
        for k, piece in enumerate(split3(norms)):
            extra = jnp.where(lanes == k, piece, extra)
        o_ref[rows + j * step:rows + (j + 1) * step, :] = extra.astype(jnp.bfloat16)


def modes_kernel(mine_ref, other_ref, s_ref, y_ref, o_ref, e_ref, *, nf, nb, nm, nv, nx):
    nvx = nv * nx
    first = owned_half() == 0
    mine = mine_ref[...].astype(jnp.float32)
    other = other_ref[...].astype(jnp.float32)
    halves = (jnp.where(first, mine, other), jnp.where(first, other, mine))
    rows = mine.shape[0] // 2
    low = lax.broadcasted_iota(jnp.int32, (nm, 2 * nb), 1) < nb
    lane = lax.broadcasted_iota(jnp.int32, (nm, nf), 1)
    energy = jnp.zeros((nm, nf), jnp.float32)
    for f in range(nf):
        part = halves[f // (nf // 2)]
        at = (f % (nf // 2)) * nm
        coef = part[at:at + nm]
        extra = part[rows + at:rows + at + nm]
        energy = jnp.where(lane == f, extra[:, 0:1] + extra[:, 1:2] + extra[:, 2:3], energy)
        left = jnp.concatenate([jnp.where(low, coef, -coef), pltpu.roll(coef, nb, 1)], axis=0)
        m = jnp.dot(left.astype(jnp.bfloat16), y_ref[2 * nb * f:2 * nb * (f + 1), :],
                    preferred_element_type=jnp.float32)
        base = f * 2 * nm * nvx
        for c in range(nvx):
            v = c // nx
            o_ref[pl.ds(base + c, 2 * nm, stride=nvx), :] = (
                m[:, c * 128:(c + 1) * 128] * s_ref[v:v + 1, :])
    e_ref[...] = jnp.sqrt(energy / nb)


def shards(snapshots, quad_weight, mode_guess, bins, starts):
    nt, nv, nx, ny = snapshots.shape
    nf, nb, _, nm = mode_guess.shape
    nvx = nv * nx
    grid_points = nx * ny * lax.axis_size(SX) * lax.axis_size(SY)
    vmem = pl.BlockSpec(memory_space=pltpu.VMEM)
    hbm = pl.BlockSpec(memory_space=pltpu.HBM)
    params = pltpu.CompilerParams(vmem_limit_bytes=40 * MIB)

    x = snapshots.reshape(nt * nvx, ny)
    guess = jnp.transpose(mode_guess, (0, 2, 3, 1))
    nchunk = 4
    packed = nf // 2 * nv * nm + TAIL
    y, mine, other = pl.pallas_call(
        functools.partial(local_kernel, nf=nf, nb=nb, nt=nt, nm=nm, nv=nv, nx=nx),
        out_shape=(jax.ShapeDtypeStruct((nf * 2 * nb, nvx * ny), jnp.bfloat16),
                   jax.ShapeDtypeStruct((packed, 128), jnp.bfloat16),
                   jax.ShapeDtypeStruct((packed, 128), jnp.bfloat16)),
        in_specs=[hbm] * 5,
        out_specs=(vmem, vmem, vmem),
        scratch_shapes=[
            pltpu.VMEM((nchunk, nt * nvx // nchunk, ny), jnp.bfloat16),
            pltpu.VMEM((nt * nvx, ny), jnp.float32),
            pltpu.VMEM((nt, nvx * ny), jnp.bfloat16),
            pltpu.VMEM((nf * nv * nm, 128), jnp.bfloat16),
            pltpu.VMEM((nv, nx, ny), jnp.float32),
            pltpu.VMEM((nf, 2, nm, nb), jnp.float32),
            pltpu.VMEM((nb, 128), jnp.int32),
            pltpu.VMEM((nf + 8, 128), jnp.int32),
            pltpu.VMEM((2, nf + 8, nt), jnp.float32),
            pltpu.VMEM((2, nb, 128), jnp.float32),
            pltpu.VMEM((nb, nt), jnp.float32),
            pltpu.VMEM((2, 4 * nb, nt), jnp.bfloat16),
            pltpu.SMEM((nb,), jnp.int32),
            pltpu.SMEM((nf,), jnp.int32),
            pltpu.SemaphoreType.DMA((4 + nchunk,)),
        ],
        compiler_params=params,
        name="local_part",
    )(*[pltpu.with_memory_space_constraint(a, pltpu.HBM) for a in (starts, bins, x, quad_weight, guess)])
    swap = ((0, 1), (1, 0))
    received = [lax.ppermute(other, CORE, swap)]
    for step in STEPS + (LAST,):
        mine = pl.pallas_call(
            add_kernel,
            out_shape=jax.ShapeDtypeStruct((packed, 128), jnp.bfloat16),
            in_specs=[vmem] * (1 + len(received)), out_specs=vmem, compiler_params=params,
            name="add_partials",
        )(mine, *received)
        moves = [step] if len(step) == 1 else [step[:1], step[1:], step]
        received = [lax.ppermute(mine, AXES, flip_pairs(*move)) for move in moves]
    coef, scale = pl.pallas_call(
        functools.partial(owner_kernel, nv=nv, nm=nm, count=float(nt * grid_points),
                          denom=float(nv * grid_points)),
        out_shape=(jax.ShapeDtypeStruct((nf * nm, 128), jnp.bfloat16),
                   jax.ShapeDtypeStruct((8, 128), jnp.float32)),
        in_specs=[vmem, vmem], out_specs=(vmem, vmem), compiler_params=params, name="owner_part",
    )(mine, *received)
    coef_other = lax.ppermute(coef, CORE, swap)
    modes, energy = pl.pallas_call(
        functools.partial(modes_kernel, nf=nf, nb=nb, nm=nm, nv=nv, nx=nx),
        out_shape=(jax.ShapeDtypeStruct((nf * 2 * nm * nvx, ny), jnp.float32),
                   jax.ShapeDtypeStruct((nm, nf), jnp.float32)),
        in_specs=[vmem] * 4, out_specs=(vmem, vmem), compiler_params=params,
        name="modes_part",
    )(coef, coef_other, scale, y)
    return modes.reshape(nf, 2, nm, nv, nx, ny), energy.T


def solution(mesh):
    finer = Mesh(mesh.devices.reshape(SIZES), AXES)
    placed = (P(None, None, SX, SY), P(None, SX, SY), P(), P(), P())
    return jax.shard_map(
        shards,
        mesh=finer,
        in_specs=placed,
        out_specs=(P(None, None, None, None, SX, SY), P()),
        check_vma=False,
    )
```

```python
import functools
import math

import jax
import jax.numpy as jnp
from jax import lax
from jax.experimental import pallas as pl
from jax.experimental.pallas import tpu as pltpu
from jax.sharding import Mesh
from jax.sharding import PartitionSpec as P
import numpy as np

NFFT = 256
EPS = 1e-06
AXES = ("sx_0", "sx_1", "sx_2", "sy_0", "sy_1")
SX = AXES[:3]
SY = AXES[3:]
SIZES = (2, 4, 4, 4, 2)
STEPS = (((1, 1), (2, 1)), ((1, 3), (2, 3)), ((0, 1), (3, 1)))
LAST = ((3, 3),)
CORE = "sy_1"
MIB = 1 << 20


def flip_pairs(*flips):
    pairs = []
    for at in np.ndindex(*SIZES):
        to = list(at)
        for axis, mask in flips:
            to[axis] ^= mask
            to[-1] ^= 1
        pairs.append((int(np.ravel_multi_index(at, SIZES)), int(np.ravel_multi_index(to, SIZES))))
    return pairs


def owned_half():
    total = lax.axis_index(AXES[0])
    for name in AXES[1:]:
        total = total + lax.axis_index(name)
    return total & 1


def split3(x):
    hi = x.astype(jnp.bfloat16).astype(jnp.float32)
    mid = (x - hi).astype(jnp.bfloat16).astype(jnp.float32)
    lo = (x - hi - mid).astype(jnp.bfloat16).astype(jnp.float32)
    return hi, mid, lo


def split2(x):
    hi = x.astype(jnp.bfloat16)
    lo = (x - hi.astype(jnp.float32)).astype(jnp.bfloat16)
    return hi, lo


TAIL = 16


def as_rows(row):
    parts = split3(row)
    return jnp.concatenate(list(parts) + [jnp.zeros((TAIL - 3, 128), jnp.float32)], axis=0).astype(jnp.bfloat16)


def from_rows(tile):
    return tile[0:1] + tile[1:2] + tile[2:3]


def local_kernel(starts_hbm, bins_hbm, x_hbm, w_hbm, g_hbm, y_ref, mine_ref, other_ref,
                 xb, xf, xs, zall, wv, gv, st, bn, ta, tb, win, amat, starts_ref, bins_ref, sems,
                 *, nf, nb, nt, nm, nv, nx):
    nvx = nv * nx
    rows = nt * nvx
    own = owned_half()
    nchunk = xb.shape[0]
    chunk = rows // nchunk

    copies = [pltpu.make_async_copy(starts_hbm, starts_ref, sems.at[0]),
              pltpu.make_async_copy(bins_hbm, bins_ref, sems.at[1]),
              pltpu.make_async_copy(w_hbm, wv, sems.at[2]),
              pltpu.make_async_copy(g_hbm, gv, sems.at[3])]
    pieces = [pltpu.make_async_copy(x_hbm.at[pl.ds(i * chunk, chunk)], xb.at[i], sems.at[4 + i])
              for i in range(nchunk)]
    for c in copies[:2] + pieces + copies[2:]:
        c.start()
    copies[0].wait()
    copies[1].wait()

    lane = lax.broadcasted_iota(jnp.int32, (1, 128), 1)
    for b in range(nb):
        st[b:b + 1, :] = jnp.full((1, 128), starts_ref[b], jnp.int32)
    for f in range(nf):
        bn[f:f + 1, :] = jnp.full((1, 128), bins_ref[f], jnp.int32)
    bn[nf:nf + 8, :] = jnp.ones((8, 128), jnp.int32)
    unit = 2.0 * math.pi / NFFT
    times = lax.broadcasted_iota(jnp.int32, (nf + 8, nt), 1)
    phase = ((bn[:, :1] * times) & (NFFT - 1)).astype(jnp.float32) * unit
    ta[0] = jnp.cos(phase)
    ta[1] = jnp.sin(phase)
    bin_lane = jnp.ones((1, 128), jnp.int32)
    for f in range(nf):
        bin_lane = jnp.where(lane == f, bins_ref[f], bin_lane)
    phase_b = ((st[:, :1] * bin_lane) & (NFFT - 1)).astype(jnp.float32) * unit
    tb[0] = jnp.cos(phase_b)
    tb[1] = jnp.sin(phase_b)
    norm_c = 1.0 / math.sqrt(sum((0.5 - 0.5 * math.cos(unit * t)) ** 2 for t in range(NFFT)))
    since = lax.broadcasted_iota(jnp.int32, (nb, nt), 1) - st[:, :1]
    cosd = ta[0, nf:nf + 1, :] * tb[0, :, nf:nf + 1] + ta[1, nf:nf + 1, :] * tb[1, :, nf:nf + 1]
    inside = (since >= 0) & (since < NFFT)
    win[...] = jnp.where(inside, norm_c * (0.5 - 0.5 * cosd), 0.0)

    for i in range(nchunk):
        pieces[i].wait()
        xf[i * chunk:(i + 1) * chunk, :] = xb[i].astype(jnp.float32)
    copies[2].wait()
    copies[3].wait()
    low = lax.broadcasted_iota(jnp.int32, (nm, 2 * nb), 1) < nb
    sqrt_w = jnp.concatenate([jnp.sqrt(wv[c // nx, c % nx:c % nx + 1, :]) for c in range(nvx)], axis=1)
    span = nx * 128
    zeros = jnp.zeros((2 * nm, 2 * nb), jnp.float32)

    def build(j):
        slot = j % 2
        for i in range(2):
            f = 2 * j + i
            ca = ta[0, f:f + 1, :]
            sa = ta[1, f:f + 1, :]
            cb = tb[0, :, f:f + 1]
            sb = tb[1, :, f:f + 1]
            ww = win[...]
            base = i * 2 * nb
            amat[slot, base:base + nb, :] = (ww * (ca * cb + sa * sb)).astype(jnp.bfloat16)
            amat[slot, base + nb:base + 2 * nb, :] = (ww * (ca * sb - sa * cb)).astype(jnp.bfloat16)

    def transform(j, v):
        cols = slice(v * span, (v + 1) * span)
        q = jnp.dot(amat[j % 2], xs[:, cols], preferred_element_type=jnp.float32)
        y_ref[4 * nb * j:4 * nb * (j + 1), cols] = (q * sqrt_w[:, cols]).astype(jnp.bfloat16)

    def project(j):
        yf = y_ref[4 * nb * j:4 * nb * (j + 1), :]
        both = []
        for i in range(2):
            pr = gv[2 * j + i, 0]
            pi = gv[2 * j + i, 1]
            guess = jnp.concatenate([jnp.concatenate([pr, -pi], axis=1),
                                     jnp.concatenate([pi, pr], axis=1)], axis=0)
            both.append(jnp.concatenate([guess, zeros] if i == 0 else [zeros, guess], axis=1))
        ghi, glo = split2(jnp.concatenate(both, axis=0))
        proj = jnp.dot(jnp.concatenate([ghi, glo], axis=0), yf, preferred_element_type=jnp.float32)
        proj = proj[:4 * nm] + proj[4 * nm:]
        phi, plo = split2(proj)
        pst = jnp.concatenate([phi, plo], axis=0)
        zs = [[], []]
        for v in range(nv):
            r = lax.dot_general(pst[:, v * span:(v + 1) * span], yf[:, v * span:(v + 1) * span],
                                (((1,), (1,)), ((), ())), preferred_element_type=jnp.float32)
            r = r[:4 * nm] + r[4 * nm:]
            for i in range(2):
                part = r[i * 2 * nm:(i + 1) * 2 * nm, i * 2 * nb:(i + 1) * 2 * nb]
                ru = part[:nm]
                rv = pltpu.roll(part[nm:], nb, 1)
                zs[i].append(jnp.where(low, ru, -ru) + rv)
        base = j * nv * 2 * nm
        for v in range(nv):
            block = jnp.concatenate([zs[0][v], zs[1][v]], axis=0).astype(jnp.bfloat16)
            zall[base + v * 2 * nm:base + (v + 1) * 2 * nm, :] = block

    build(0)
    sums = []
    for v in range(nv):
        acc = jnp.zeros((1, 128), jnp.float32)
        for k in range(nx):
            col = v * nx + k
            part = xf[pl.ds(col, nt, stride=nvx), :]
            xs[:, col * 128:(col + 1) * 128] = part.astype(jnp.bfloat16)
            sq = jnp.sum(part * part, axis=0, keepdims=True)
            acc = acc + sq * wv[v, k:k + 1, :]
        sums.append(jnp.sum(acc, axis=1, keepdims=True))
        transform(0, v)
    msq = jnp.zeros((1, 128), jnp.float32)
    for v in range(nv):
        msq = jnp.where(lane == v, sums[v], msq)
    tail = as_rows(msq)
    mine_ref[mine_ref.shape[0] - TAIL:, :] = tail
    other_ref[other_ref.shape[0] - TAIL:, :] = tail
    for j in range(1, nf // 2):
        build(j)
        for v in range(nv):
            transform(j, v)
        project(j - 1)
    project(nf // 2 - 1)
    cut = nf // 2 * nv * nm
    low_half = zall[:cut, :].astype(jnp.float32)
    high_half = zall[cut:, :].astype(jnp.float32)
    mine_ref[:cut, :] = jnp.where(own == 0, low_half, high_half).astype(jnp.bfloat16)
    other_ref[:cut, :] = jnp.where(own == 0, high_half, low_half).astype(jnp.bfloat16)


def add_kernel(*refs):
    o_ref = refs[-1]
    cut = o_ref.shape[0] - TAIL
    terms = [r[...].astype(jnp.float32) for r in refs[:-1]]
    while len(terms) > 1:
        terms = [terms[i] + terms[i + 1] for i in range(0, len(terms), 2)]
    total = terms[0]
    o_ref[:cut, :] = total[:cut].astype(jnp.bfloat16)
    o_ref[cut:, :] = as_rows(from_rows(total[cut:]))


def owner_kernel(a_ref, b_ref, o_ref, s_ref, *, nv, nm, count, denom):
    cut = a_ref.shape[0] - TAIL
    total = a_ref[...].astype(jnp.float32) + b_ref[...].astype(jnp.float32)
    msq = from_rows(total[cut:])
    scales = []
    for v in range(nv):
        scale = lax.rsqrt(jnp.broadcast_to(msq[:, v:v + 1], (1, 128)) / count + EPS)
        s_ref[v:v + 1, :] = scale
        scales.append(scale * scale)
    s_ref[nv:, :] = jnp.zeros((8 - nv, 128), jnp.float32)
    step = 2 * nm
    lanes = lax.broadcasted_iota(jnp.int32, (step, 128), 1)
    rows = cut // nv
    for j in range(rows // step):
        z = jnp.zeros((step, 128), jnp.float32)
        for v in range(nv):
            base = (j * nv + v) * step
            z = z + total[base:base + step] * scales[v]
        z = z / denom
        norms = jnp.sum(z * z, axis=1, keepdims=True)
        o_ref[j * step:(j + 1) * step, :] = (z * lax.rsqrt(norms + EPS)).astype(jnp.bfloat16)
        extra = jnp.zeros((step, 128), jnp.float32)
        for k, piece in enumerate(split3(norms)):
            extra = jnp.where(lanes == k, piece, extra)
        o_ref[rows + j * step:rows + (j + 1) * step, :] = extra.astype(jnp.bfloat16)


def modes_kernel(mine_ref, other_ref, s_ref, y_ref, o_ref, e_ref, *, nf, nb, nm, nv, nx):
    nvx = nv * nx
    first = owned_half() == 0
    mine = mine_ref[...].astype(jnp.float32)
    other = other_ref[...].astype(jnp.float32)
    halves = (jnp.where(first, mine, other), jnp.where(first, other, mine))
    rows = mine.shape[0] // 2
    low = lax.broadcasted_iota(jnp.int32, (nm, 2 * nb), 1) < nb
    lane = lax.broadcasted_iota(jnp.int32, (nm, nf), 1)
    energy = jnp.zeros((nm, nf), jnp.float32)
    for f in range(nf):
        part = halves[f // (nf // 2)]
        at = (f % (nf // 2)) * nm
        coef = part[at:at + nm]
        extra = part[rows + at:rows + at + nm]
        energy = jnp.where(lane == f, extra[:, 0:1] + extra[:, 1:2] + extra[:, 2:3], energy)
        left = jnp.concatenate([jnp.where(low, coef, -coef), pltpu.roll(coef, nb, 1)], axis=0)
        m = jnp.dot(left.astype(jnp.bfloat16), y_ref[2 * nb * f:2 * nb * (f + 1), :],
                    preferred_element_type=jnp.float32)
        base = f * 2 * nm * nvx
        for c in range(nvx):
            v = c // nx
            o_ref[pl.ds(base + c, 2 * nm, stride=nvx), :] = (
                m[:, c * 128:(c + 1) * 128] * s_ref[v:v + 1, :])
    e_ref[...] = jnp.sqrt(energy / nb)


def shards(snapshots, quad_weight, mode_guess, bins, starts):
    nt, nv, nx, ny = snapshots.shape
    nf, nb, _, nm = mode_guess.shape
    nvx = nv * nx
    grid_points = nx * ny * lax.axis_size(SX) * lax.axis_size(SY)
    vmem = pl.BlockSpec(memory_space=pltpu.VMEM)
    hbm = pl.BlockSpec(memory_space=pltpu.HBM)
    params = pltpu.CompilerParams(vmem_limit_bytes=40 * MIB)

    x = snapshots.reshape(nt * nvx, ny)
    guess = jnp.transpose(mode_guess, (0, 2, 3, 1))
    nchunk = 4
    packed = nf // 2 * nv * nm + TAIL
    y, mine, other = pl.pallas_call(
        functools.partial(local_kernel, nf=nf, nb=nb, nt=nt, nm=nm, nv=nv, nx=nx),
        out_shape=(jax.ShapeDtypeStruct((nf * 2 * nb, nvx * ny), jnp.bfloat16),
                   jax.ShapeDtypeStruct((packed, 128), jnp.bfloat16),
                   jax.ShapeDtypeStruct((packed, 128), jnp.bfloat16)),
        in_specs=[hbm] * 5,
        out_specs=(vmem, vmem, vmem),
        scratch_shapes=[
            pltpu.VMEM((nchunk, nt * nvx // nchunk, ny), jnp.bfloat16),
            pltpu.VMEM((nt * nvx, ny), jnp.float32),
            pltpu.VMEM((nt, nvx * ny), jnp.bfloat16),
            pltpu.VMEM((nf * nv * nm, 128), jnp.bfloat16),
            pltpu.VMEM((nv, nx, ny), jnp.float32),
            pltpu.VMEM((nf, 2, nm, nb), jnp.float32),
            pltpu.VMEM((nb, 128), jnp.int32),
            pltpu.VMEM((nf + 8, 128), jnp.int32),
            pltpu.VMEM((2, nf + 8, nt), jnp.float32),
            pltpu.VMEM((2, nb, 128), jnp.float32),
            pltpu.VMEM((nb, nt), jnp.float32),
            pltpu.VMEM((2, 4 * nb, nt), jnp.bfloat16),
            pltpu.SMEM((nb,), jnp.int32),
            pltpu.SMEM((nf,), jnp.int32),
            pltpu.SemaphoreType.DMA((4 + nchunk,)),
        ],
        compiler_params=params,
        name="local_part",
    )(*[pltpu.with_memory_space_constraint(a, pltpu.HBM) for a in (starts, bins, x, quad_weight, guess)])
    swap = ((0, 1), (1, 0))
    received = [lax.ppermute(other, CORE, swap)]
    for step in STEPS + (LAST,):
        mine = pl.pallas_call(
            add_kernel,
            out_shape=jax.ShapeDtypeStruct((packed, 128), jnp.bfloat16),
            in_specs=[vmem] * (1 + len(received)), out_specs=vmem, compiler_params=params,
            name="add_partials",
        )(mine, *received)
        moves = [step] if len(step) == 1 else [step[:1], step[1:], step]
        received = [lax.ppermute(mine, AXES, flip_pairs(*move)) for move in moves]
    coef, scale = pl.pallas_call(
        functools.partial(owner_kernel, nv=nv, nm=nm, count=float(nt * grid_points),
                          denom=float(nv * grid_points)),
        out_shape=(jax.ShapeDtypeStruct((nf * nm, 128), jnp.bfloat16),
                   jax.ShapeDtypeStruct((8, 128), jnp.float32)),
        in_specs=[vmem, vmem], out_specs=(vmem, vmem), compiler_params=params, name="owner_part",
    )(mine, *received)
    coef_other = lax.ppermute(coef, CORE, swap)
    modes, energy = pl.pallas_call(
        functools.partial(modes_kernel, nf=nf, nb=nb, nm=nm, nv=nv, nx=nx),
        out_shape=(jax.ShapeDtypeStruct((nf * 2 * nm * nvx, ny), jnp.float32),
                   jax.ShapeDtypeStruct((nm, nf), jnp.float32)),
        in_specs=[vmem] * 4, out_specs=(vmem, vmem), compiler_params=params,
        name="modes_part",
    )(coef, coef_other, scale, y)
    return modes.reshape(nf, 2, nm, nv, nx, ny), energy.T


def solution(mesh):
    finer = Mesh(mesh.devices.reshape(SIZES), AXES)
    placed = (P(None, None, SX, SY), P(None, SX, SY), P(), P(), P())
    return jax.shard_map(
        shards,
        mesh=finer,
        in_specs=placed,
        out_specs=(P(None, None, None, None, SX, SY), P()),
        check_vma=False,
    )
```

```python
import functools
import math

import jax
import jax.numpy as jnp
from jax import lax
from jax.experimental import pallas as pl
from jax.experimental.pallas import tpu as pltpu
from jax.sharding import Mesh
from jax.sharding import PartitionSpec as P
import numpy as np

NFFT = 256
EPS = 1e-06
AXES = ("sx_0", "sx_1", "sx_2", "sy_0", "sy_1")
SX = AXES[:3]
SY = AXES[3:]
SIZES = (2, 4, 4, 4, 2)
STEPS = (((0, 1), (3, 1)), ((1, 1), (2, 1)), ((1, 3), (2, 3)))
LAST = ((3, 3),)
CORE = "sy_1"
MIB = 1 << 20


def flip_pairs(*flips):
    pairs = []
    for at in np.ndindex(*SIZES):
        to = list(at)
        for axis, mask in flips:
            to[axis] ^= mask
            to[-1] ^= 1
        pairs.append((int(np.ravel_multi_index(at, SIZES)), int(np.ravel_multi_index(to, SIZES))))
    return pairs


def owned_half():
    total = lax.axis_index(AXES[0])
    for name in AXES[1:]:
        total = total + lax.axis_index(name)
    return total & 1


def split3(x):
    hi = x.astype(jnp.bfloat16).astype(jnp.float32)
    mid = (x - hi).astype(jnp.bfloat16).astype(jnp.float32)
    lo = (x - hi - mid).astype(jnp.bfloat16).astype(jnp.float32)
    return hi, mid, lo


def split2(x):
    hi = x.astype(jnp.bfloat16)
    lo = (x - hi.astype(jnp.float32)).astype(jnp.bfloat16)
    return hi, lo


TAIL = 16


def as_rows(row):
    parts = split3(row)
    return jnp.concatenate(list(parts) + [jnp.zeros((TAIL - 3, 128), jnp.float32)], axis=0).astype(jnp.bfloat16)


def from_rows(tile):
    return tile[0:1] + tile[1:2] + tile[2:3]


def local_kernel(starts_hbm, bins_hbm, x_hbm, w_hbm, g_hbm, y_ref, mine_ref, other_ref,
                 xb, xf, xs, zall, wv, gv, st, bn, ta, tb, win, amat, starts_ref, bins_ref, sems,
                 *, nf, nb, nt, nm, nv, nx):
    nvx = nv * nx
    rows = nt * nvx
    own = owned_half()
    nchunk = xb.shape[0]
    chunk = rows // nchunk

    copies = [pltpu.make_async_copy(starts_hbm, starts_ref, sems.at[0]),
              pltpu.make_async_copy(bins_hbm, bins_ref, sems.at[1]),
              pltpu.make_async_copy(w_hbm, wv, sems.at[2]),
              pltpu.make_async_copy(g_hbm, gv, sems.at[3])]
    pieces = [pltpu.make_async_copy(x_hbm.at[pl.ds(i * chunk, chunk)], xb.at[i], sems.at[4 + i])
              for i in range(nchunk)]
    for c in copies[:2] + pieces + copies[2:]:
        c.start()
    copies[0].wait()
    copies[1].wait()

    lane = lax.broadcasted_iota(jnp.int32, (1, 128), 1)
    for b in range(nb):
        st[b:b + 1, :] = jnp.full((1, 128), starts_ref[b], jnp.int32)
    for f in range(nf):
        bn[f:f + 1, :] = jnp.full((1, 128), bins_ref[f], jnp.int32)
    bn[nf:nf + 8, :] = jnp.ones((8, 128), jnp.int32)
    unit = 2.0 * math.pi / NFFT
    times = lax.broadcasted_iota(jnp.int32, (nf + 8, nt), 1)
    phase = ((bn[:, :1] * times) & (NFFT - 1)).astype(jnp.float32) * unit
    ta[0] = jnp.cos(phase)
    ta[1] = jnp.sin(phase)
    bin_lane = jnp.ones((1, 128), jnp.int32)
    for f in range(nf):
        bin_lane = jnp.where(lane == f, bins_ref[f], bin_lane)
    phase_b = ((st[:, :1] * bin_lane) & (NFFT - 1)).astype(jnp.float32) * unit
    tb[0] = jnp.cos(phase_b)
    tb[1] = jnp.sin(phase_b)
    norm_c = 1.0 / math.sqrt(sum((0.5 - 0.5 * math.cos(unit * t)) ** 2 for t in range(NFFT)))
    since = lax.broadcasted_iota(jnp.int32, (nb, nt), 1) - st[:, :1]
    cosd = ta[0, nf:nf + 1, :] * tb[0, :, nf:nf + 1] + ta[1, nf:nf + 1, :] * tb[1, :, nf:nf + 1]
    inside = (since >= 0) & (since < NFFT)
    win[...] = jnp.where(inside, norm_c * (0.5 - 0.5 * cosd), 0.0)

    for i in range(nchunk):
        pieces[i].wait()
        xf[i * chunk:(i + 1) * chunk, :] = xb[i].astype(jnp.float32)
    copies[2].wait()
    copies[3].wait()
    low = lax.broadcasted_iota(jnp.int32, (nm, 2 * nb), 1) < nb
    sqrt_w = jnp.concatenate([jnp.sqrt(wv[c // nx, c % nx:c % nx + 1, :]) for c in range(nvx)], axis=1)
    span = nx * 128
    zeros = jnp.zeros((2 * nm, 2 * nb), jnp.float32)

    def build(j):
        slot = j % 2
        for i in range(2):
            f = 2 * j + i
            ca = ta[0, f:f + 1, :]
            sa = ta[1, f:f + 1, :]
            cb = tb[0, :, f:f + 1]
            sb = tb[1, :, f:f + 1]
            ww = win[...]
            base = i * 2 * nb
            amat[slot, base:base + nb, :] = (ww * (ca * cb + sa * sb)).astype(jnp.bfloat16)
            amat[slot, base + nb:base + 2 * nb, :] = (ww * (ca * sb - sa * cb)).astype(jnp.bfloat16)

    def transform(j, v):
        cols = slice(v * span, (v + 1) * span)
        q = jnp.dot(amat[j % 2], xs[:, cols], preferred_element_type=jnp.float32)
        y_ref[4 * nb * j:4 * nb * (j + 1), cols] = (q * sqrt_w[:, cols]).astype(jnp.bfloat16)

    def project(j):
        yf = y_ref[4 * nb * j:4 * nb * (j + 1), :]
        both = []
        for i in range(2):
            pr = gv[2 * j + i, 0]
            pi = gv[2 * j + i, 1]
            guess = jnp.concatenate([jnp.concatenate([pr, -pi], axis=1),
                                     jnp.concatenate([pi, pr], axis=1)], axis=0)
            both.append(jnp.concatenate([guess, zeros] if i == 0 else [zeros, guess], axis=1))
        ghi, glo = split2(jnp.concatenate(both, axis=0))
        proj = jnp.dot(jnp.concatenate([ghi, glo], axis=0), yf, preferred_element_type=jnp.float32)
        proj = proj[:4 * nm] + proj[4 * nm:]
        phi, plo = split2(proj)
        pst = jnp.concatenate([phi, plo], axis=0)
        zs = [[], []]
        for v in range(nv):
            r = lax.dot_general(pst[:, v * span:(v + 1) * span], yf[:, v * span:(v + 1) * span],
                                (((1,), (1,)), ((), ())), preferred_element_type=jnp.float32)
            r = r[:4 * nm] + r[4 * nm:]
            for i in range(2):
                part = r[i * 2 * nm:(i + 1) * 2 * nm, i * 2 * nb:(i + 1) * 2 * nb]
                ru = part[:nm]
                rv = pltpu.roll(part[nm:], nb, 1)
                zs[i].append(jnp.where(low, ru, -ru) + rv)
        base = j * nv * 2 * nm
        for v in range(nv):
            block = jnp.concatenate([zs[0][v], zs[1][v]], axis=0).astype(jnp.bfloat16)
            zall[base + v * 2 * nm:base + (v + 1) * 2 * nm, :] = block

    build(0)
    sums = []
    for v in range(nv):
        acc = jnp.zeros((1, 128), jnp.float32)
        for k in range(nx):
            col = v * nx + k
            part = xf[pl.ds(col, nt, stride=nvx), :]
            xs[:, col * 128:(col + 1) * 128] = part.astype(jnp.bfloat16)
            sq = jnp.sum(part * part, axis=0, keepdims=True)
            acc = acc + sq * wv[v, k:k + 1, :]
        sums.append(jnp.sum(acc, axis=1, keepdims=True))
        transform(0, v)
    msq = jnp.zeros((1, 128), jnp.float32)
    for v in range(nv):
        msq = jnp.where(lane == v, sums[v], msq)
    tail = as_rows(msq)
    mine_ref[mine_ref.shape[0] - TAIL:, :] = tail
    other_ref[other_ref.shape[0] - TAIL:, :] = tail
    for j in range(1, nf // 2):
        build(j)
        for v in range(nv):
            transform(j, v)
        project(j - 1)
    project(nf // 2 - 1)
    cut = nf // 2 * nv * nm
    low_half = zall[:cut, :].astype(jnp.float32)
    high_half = zall[cut:, :].astype(jnp.float32)
    mine_ref[:cut, :] = jnp.where(own == 0, low_half, high_half).astype(jnp.bfloat16)
    other_ref[:cut, :] = jnp.where(own == 0, high_half, low_half).astype(jnp.bfloat16)


def add_kernel(*refs):
    o_ref = refs[-1]
    cut = o_ref.shape[0] - TAIL
    terms = [r[...].astype(jnp.float32) for r in refs[:-1]]
    while len(terms) > 1:
        terms = [terms[i] + terms[i + 1] for i in range(0, len(terms), 2)]
    total = terms[0]
    o_ref[:cut, :] = total[:cut].astype(jnp.bfloat16)
    o_ref[cut:, :] = as_rows(from_rows(total[cut:]))


def owner_kernel(a_ref, b_ref, o_ref, s_ref, *, nv, nm, count, denom):
    cut = a_ref.shape[0] - TAIL
    total = a_ref[...].astype(jnp.float32) + b_ref[...].astype(jnp.float32)
    msq = from_rows(total[cut:])
    scales = []
    for v in range(nv):
        scale = lax.rsqrt(jnp.broadcast_to(msq[:, v:v + 1], (1, 128)) / count + EPS)
        s_ref[v:v + 1, :] = scale
        scales.append(scale * scale)
    s_ref[nv:, :] = jnp.zeros((8 - nv, 128), jnp.float32)
    step = 2 * nm
    lanes = lax.broadcasted_iota(jnp.int32, (step, 128), 1)
    rows = cut // nv
    for j in range(rows // step):
        z = jnp.zeros((step, 128), jnp.float32)
        for v in range(nv):
            base = (j * nv + v) * step
            z = z + total[base:base + step] * scales[v]
        z = z / denom
        norms = jnp.sum(z * z, axis=1, keepdims=True)
        o_ref[j * step:(j + 1) * step, :] = (z * lax.rsqrt(norms + EPS)).astype(jnp.bfloat16)
        extra = jnp.zeros((step, 128), jnp.float32)
        for k, piece in enumerate(split3(norms)):
            extra = jnp.where(lanes == k, piece, extra)
        o_ref[rows + j * step:rows + (j + 1) * step, :] = extra.astype(jnp.bfloat16)


def modes_kernel(mine_ref, other_ref, s_ref, y_ref, o_ref, e_ref, *, nf, nb, nm, nv, nx):
    nvx = nv * nx
    first = owned_half() == 0
    mine = mine_ref[...].astype(jnp.float32)
    other = other_ref[...].astype(jnp.float32)
    halves = (jnp.where(first, mine, other), jnp.where(first, other, mine))
    rows = mine.shape[0] // 2
    low = lax.broadcasted_iota(jnp.int32, (nm, 2 * nb), 1) < nb
    lane = lax.broadcasted_iota(jnp.int32, (nm, nf), 1)
    energy = jnp.zeros((nm, nf), jnp.float32)
    for f in range(nf):
        part = halves[f // (nf // 2)]
        at = (f % (nf // 2)) * nm
        coef = part[at:at + nm]
        extra = part[rows + at:rows + at + nm]
        energy = jnp.where(lane == f, extra[:, 0:1] + extra[:, 1:2] + extra[:, 2:3], energy)
        left = jnp.concatenate([jnp.where(low, coef, -coef), pltpu.roll(coef, nb, 1)], axis=0)
        m = jnp.dot(left.astype(jnp.bfloat16), y_ref[2 * nb * f:2 * nb * (f + 1), :],
                    preferred_element_type=jnp.float32)
        base = f * 2 * nm * nvx
        for c in range(nvx):
            v = c // nx
            o_ref[pl.ds(base + c, 2 * nm, stride=nvx), :] = (
                m[:, c * 128:(c + 1) * 128] * s_ref[v:v + 1, :])
    e_ref[...] = jnp.sqrt(energy / nb)


def shards(snapshots, quad_weight, mode_guess, bins, starts):
    nt, nv, nx, ny = snapshots.shape
    nf, nb, _, nm = mode_guess.shape
    nvx = nv * nx
    grid_points = nx * ny * lax.axis_size(SX) * lax.axis_size(SY)
    vmem = pl.BlockSpec(memory_space=pltpu.VMEM)
    hbm = pl.BlockSpec(memory_space=pltpu.HBM)
    params = pltpu.CompilerParams(vmem_limit_bytes=40 * MIB)

    x = snapshots.reshape(nt * nvx, ny)
    guess = jnp.transpose(mode_guess, (0, 2, 3, 1))
    nchunk = 4
    packed = nf // 2 * nv * nm + TAIL
    y, mine, other = pl.pallas_call(
        functools.partial(local_kernel, nf=nf, nb=nb, nt=nt, nm=nm, nv=nv, nx=nx),
        out_shape=(jax.ShapeDtypeStruct((nf * 2 * nb, nvx * ny), jnp.bfloat16),
                   jax.ShapeDtypeStruct((packed, 128), jnp.bfloat16),
                   jax.ShapeDtypeStruct((packed, 128), jnp.bfloat16)),
        in_specs=[hbm] * 5,
        out_specs=(vmem, vmem, vmem),
        scratch_shapes=[
            pltpu.VMEM((nchunk, nt * nvx // nchunk, ny), jnp.bfloat16),
            pltpu.VMEM((nt * nvx, ny), jnp.float32),
            pltpu.VMEM((nt, nvx * ny), jnp.bfloat16),
            pltpu.VMEM((nf * nv * nm, 128), jnp.bfloat16),
            pltpu.VMEM((nv, nx, ny), jnp.float32),
            pltpu.VMEM((nf, 2, nm, nb), jnp.float32),
            pltpu.VMEM((nb, 128), jnp.int32),
            pltpu.VMEM((nf + 8, 128), jnp.int32),
            pltpu.VMEM((2, nf + 8, nt), jnp.float32),
            pltpu.VMEM((2, nb, 128), jnp.float32),
            pltpu.VMEM((nb, nt), jnp.float32),
            pltpu.VMEM((2, 4 * nb, nt), jnp.bfloat16),
            pltpu.SMEM((nb,), jnp.int32),
            pltpu.SMEM((nf,), jnp.int32),
            pltpu.SemaphoreType.DMA((4 + nchunk,)),
        ],
        compiler_params=params,
        name="local_part",
    )(*[pltpu.with_memory_space_constraint(a, pltpu.HBM) for a in (starts, bins, x, quad_weight, guess)])
    swap = ((0, 1), (1, 0))
    received = [lax.ppermute(other, CORE, swap)]
    for step in STEPS + (LAST,):
        mine = pl.pallas_call(
            add_kernel,
            out_shape=jax.ShapeDtypeStruct((packed, 128), jnp.bfloat16),
            in_specs=[vmem] * (1 + len(received)), out_specs=vmem, compiler_params=params,
            name="add_partials",
        )(mine, *received)
        moves = [step] if len(step) == 1 else [step[:1], step[1:], step]
        received = [lax.ppermute(mine, AXES, flip_pairs(*move)) for move in moves]
    coef, scale = pl.pallas_call(
        functools.partial(owner_kernel, nv=nv, nm=nm, count=float(nt * grid_points),
                          denom=float(nv * grid_points)),
        out_shape=(jax.ShapeDtypeStruct((nf * nm, 128), jnp.bfloat16),
                   jax.ShapeDtypeStruct((8, 128), jnp.float32)),
        in_specs=[vmem, vmem], out_specs=(vmem, vmem), compiler_params=params, name="owner_part",
    )(mine, *received)
    coef_other = lax.ppermute(coef, CORE, swap)
    modes, energy = pl.pallas_call(
        functools.partial(modes_kernel, nf=nf, nb=nb, nm=nm, nv=nv, nx=nx),
        out_shape=(jax.ShapeDtypeStruct((nf * 2 * nm * nvx, ny), jnp.float32),
                   jax.ShapeDtypeStruct((nm, nf), jnp.float32)),
        in_specs=[vmem] * 4, out_specs=(vmem, vmem), compiler_params=params,
        name="modes_part",
    )(coef, coef_other, scale, y)
    return modes.reshape(nf, 2, nm, nv, nx, ny), energy.T


def solution(mesh):
    finer = Mesh(mesh.devices.reshape(SIZES), AXES)
    placed = (P(None, None, SX, SY), P(None, SX, SY), P(), P(), P())
    return jax.shard_map(
        shards,
        mesh=finer,
        in_specs=placed,
        out_specs=(P(None, None, None, None, SX, SY), P()),
        check_vma=False,
    )
```

```python
import functools
import math

import jax
import jax.numpy as jnp
from jax import lax
from jax.experimental import pallas as pl
from jax.experimental.pallas import tpu as pltpu
from jax.sharding import Mesh
from jax.sharding import PartitionSpec as P
import numpy as np

NFFT = 256
EPS = 1e-06
AXES = ("sx_0", "sx_1", "sx_2", "sy_0", "sy_1")
SX = AXES[:3]
SY = AXES[3:]
SIZES = (2, 4, 4, 4, 2)
STEPS = (((0, 1), (3, 1)), ((1, 1), (1, 3)), ((2, 1), (2, 3)))
LAST = ((3, 3),)
CORE = "sy_1"
MIB = 1 << 20


def flip_pairs(*flips):
    pairs = []
    for at in np.ndindex(*SIZES):
        to = list(at)
        for axis, mask in flips:
            to[axis] ^= mask
            to[-1] ^= 1
        pairs.append((int(np.ravel_multi_index(at, SIZES)), int(np.ravel_multi_index(to, SIZES))))
    return pairs


def owned_half():
    total = lax.axis_index(AXES[0])
    for name in AXES[1:]:
        total = total + lax.axis_index(name)
    return total & 1


def split3(x):
    hi = x.astype(jnp.bfloat16).astype(jnp.float32)
    mid = (x - hi).astype(jnp.bfloat16).astype(jnp.float32)
    lo = (x - hi - mid).astype(jnp.bfloat16).astype(jnp.float32)
    return hi, mid, lo


def split2(x):
    hi = x.astype(jnp.bfloat16)
    lo = (x - hi.astype(jnp.float32)).astype(jnp.bfloat16)
    return hi, lo


TAIL = 16


def as_rows(row):
    parts = split3(row)
    return jnp.concatenate(list(parts) + [jnp.zeros((TAIL - 3, 128), jnp.float32)], axis=0).astype(jnp.bfloat16)


def from_rows(tile):
    return tile[0:1] + tile[1:2] + tile[2:3]


def local_kernel(starts_hbm, bins_hbm, x_hbm, w_hbm, g_hbm, y_ref, mine_ref, other_ref,
                 xb, xf, xs, zall, wv, gv, st, bn, ta, tb, win, amat, starts_ref, bins_ref, sems,
                 *, nf, nb, nt, nm, nv, nx):
    nvx = nv * nx
    rows = nt * nvx
    own = owned_half()
    nchunk = xb.shape[0]
    chunk = rows // nchunk

    copies = [pltpu.make_async_copy(starts_hbm, starts_ref, sems.at[0]),
              pltpu.make_async_copy(bins_hbm, bins_ref, sems.at[1]),
              pltpu.make_async_copy(w_hbm, wv, sems.at[2]),
              pltpu.make_async_copy(g_hbm, gv, sems.at[3])]
    pieces = [pltpu.make_async_copy(x_hbm.at[pl.ds(i * chunk, chunk)], xb.at[i], sems.at[4 + i])
              for i in range(nchunk)]
    for c in copies[:2] + pieces + copies[2:]:
        c.start()
    copies[0].wait()
    copies[1].wait()

    lane = lax.broadcasted_iota(jnp.int32, (1, 128), 1)
    for b in range(nb):
        st[b:b + 1, :] = jnp.full((1, 128), starts_ref[b], jnp.int32)
    for f in range(nf):
        bn[f:f + 1, :] = jnp.full((1, 128), bins_ref[f], jnp.int32)
    bn[nf:nf + 8, :] = jnp.ones((8, 128), jnp.int32)
    unit = 2.0 * math.pi / NFFT
    times = lax.broadcasted_iota(jnp.int32, (nf + 8, nt), 1)
    phase = ((bn[:, :1] * times) & (NFFT - 1)).astype(jnp.float32) * unit
    ta[0] = jnp.cos(phase)
    ta[1] = jnp.sin(phase)
    bin_lane = jnp.ones((1, 128), jnp.int32)
    for f in range(nf):
        bin_lane = jnp.where(lane == f, bins_ref[f], bin_lane)
    phase_b = ((st[:, :1] * bin_lane) & (NFFT - 1)).astype(jnp.float32) * unit
    tb[0] = jnp.cos(phase_b)
    tb[1] = jnp.sin(phase_b)
    norm_c = 1.0 / math.sqrt(sum((0.5 - 0.5 * math.cos(unit * t)) ** 2 for t in range(NFFT)))
    since = lax.broadcasted_iota(jnp.int32, (nb, nt), 1) - st[:, :1]
    cosd = ta[0, nf:nf + 1, :] * tb[0, :, nf:nf + 1] + ta[1, nf:nf + 1, :] * tb[1, :, nf:nf + 1]
    inside = (since >= 0) & (since < NFFT)
    win[...] = jnp.where(inside, norm_c * (0.5 - 0.5 * cosd), 0.0)

    for i in range(nchunk):
        pieces[i].wait()
        xf[i * chunk:(i + 1) * chunk, :] = xb[i].astype(jnp.float32)
    copies[2].wait()
    copies[3].wait()
    low = lax.broadcasted_iota(jnp.int32, (nm, 2 * nb), 1) < nb
    sqrt_w = jnp.concatenate([jnp.sqrt(wv[c // nx, c % nx:c % nx + 1, :]) for c in range(nvx)], axis=1)
    span = nx * 128
    zeros = jnp.zeros((2 * nm, 2 * nb), jnp.float32)

    def build(j):
        slot = j % 2
        for i in range(2):
            f = 2 * j + i
            ca = ta[0, f:f + 1, :]
            sa = ta[1, f:f + 1, :]
            cb = tb[0, :, f:f + 1]
            sb = tb[1, :, f:f + 1]
            ww = win[...]
            base = i * 2 * nb
            amat[slot, base:base + nb, :] = (ww * (ca * cb + sa * sb)).astype(jnp.bfloat16)
            amat[slot, base + nb:base + 2 * nb, :] = (ww * (ca * sb - sa * cb)).astype(jnp.bfloat16)

    def transform(j, v):
        cols = slice(v * span, (v + 1) * span)
        q = jnp.dot(amat[j % 2], xs[:, cols], preferred_element_type=jnp.float32)
        y_ref[4 * nb * j:4 * nb * (j + 1), cols] = (q * sqrt_w[:, cols]).astype(jnp.bfloat16)

    def project(j):
        yf = y_ref[4 * nb * j:4 * nb * (j + 1), :]
        both = []
        for i in range(2):
            pr = gv[2 * j + i, 0]
            pi = gv[2 * j + i, 1]
            guess = jnp.concatenate([jnp.concatenate([pr, -pi], axis=1),
                                     jnp.concatenate([pi, pr], axis=1)], axis=0)
            both.append(jnp.concatenate([guess, zeros] if i == 0 else [zeros, guess], axis=1))
        ghi, glo = split2(jnp.concatenate(both, axis=0))
        proj = jnp.dot(jnp.concatenate([ghi, glo], axis=0), yf, preferred_element_type=jnp.float32)
        proj = proj[:4 * nm] + proj[4 * nm:]
        pst = proj.astype(jnp.bfloat16)
        zs = [[], []]
        for v in range(nv):
            r = lax.dot_general(pst[:, v * span:(v + 1) * span], yf[:, v * span:(v + 1) * span],
                                (((1,), (1,)), ((), ())), preferred_element_type=jnp.float32)
            for i in range(2):
                part = r[i * 2 * nm:(i + 1) * 2 * nm, i * 2 * nb:(i + 1) * 2 * nb]
                ru = part[:nm]
                rv = pltpu.roll(part[nm:], nb, 1)
                zs[i].append(jnp.where(low, ru, -ru) + rv)
        base = j * nv * 2 * nm
        for v in range(nv):
            block = jnp.concatenate([zs[0][v], zs[1][v]], axis=0).astype(jnp.bfloat16)
            zall[base + v * 2 * nm:base + (v + 1) * 2 * nm, :] = block

    build(0)
    sums = []
    for v in range(nv):
        acc = jnp.zeros((1, 128), jnp.float32)
        for k in range(nx):
            col = v * nx + k
            part = xf[pl.ds(col, nt, stride=nvx), :]
            xs[:, col * 128:(col + 1) * 128] = part.astype(jnp.bfloat16)
            sq = jnp.sum(part * part, axis=0, keepdims=True)
            acc = acc + sq * wv[v, k:k + 1, :]
        sums.append(jnp.sum(acc, axis=1, keepdims=True))
        transform(0, v)
    msq = jnp.zeros((1, 128), jnp.float32)
    for v in range(nv):
        msq = jnp.where(lane == v, sums[v], msq)
    tail = as_rows(msq)
    mine_ref[mine_ref.shape[0] - TAIL:, :] = tail
    other_ref[other_ref.shape[0] - TAIL:, :] = tail
    for j in range(1, nf // 2):
        build(j)
        for v in range(nv):
            transform(j, v)
        project(j - 1)
    project(nf // 2 - 1)
    cut = nf // 2 * nv * nm
    low_half = zall[:cut, :].astype(jnp.float32)
    high_half = zall[cut:, :].astype(jnp.float32)
    mine_ref[:cut, :] = jnp.where(own == 0, low_half, high_half).astype(jnp.bfloat16)
    other_ref[:cut, :] = jnp.where(own == 0, high_half, low_half).astype(jnp.bfloat16)


def add_kernel(*refs):
    o_ref = refs[-1]
    cut = o_ref.shape[0] - TAIL
    terms = [r[...].astype(jnp.float32) for r in refs[:-1]]
    while len(terms) > 1:
        terms = [terms[i] + terms[i + 1] for i in range(0, len(terms), 2)]
    total = terms[0]
    o_ref[:cut, :] = total[:cut].astype(jnp.bfloat16)
    o_ref[cut:, :] = as_rows(from_rows(total[cut:]))


def owner_kernel(a_ref, b_ref, o_ref, s_ref, *, nv, nm, count, denom):
    cut = a_ref.shape[0] - TAIL
    total = a_ref[...].astype(jnp.float32) + b_ref[...].astype(jnp.float32)
    msq = from_rows(total[cut:])
    scales = []
    for v in range(nv):
        scale = lax.rsqrt(jnp.broadcast_to(msq[:, v:v + 1], (1, 128)) / count + EPS)
        s_ref[v:v + 1, :] = scale
        scales.append(scale * scale)
    s_ref[nv:, :] = jnp.zeros((8 - nv, 128), jnp.float32)
    step = 2 * nm
    lanes = lax.broadcasted_iota(jnp.int32, (step, 128), 1)
    rows = cut // nv
    for j in range(rows // step):
        z = jnp.zeros((step, 128), jnp.float32)
        for v in range(nv):
            base = (j * nv + v) * step
            z = z + total[base:base + step] * scales[v]
        z = z / denom
        norms = jnp.sum(z * z, axis=1, keepdims=True)
        o_ref[j * step:(j + 1) * step, :] = (z * lax.rsqrt(norms + EPS)).astype(jnp.bfloat16)
        extra = jnp.zeros((step, 128), jnp.float32)
        for k, piece in enumerate(split3(norms)):
            extra = jnp.where(lanes == k, piece, extra)
        o_ref[rows + j * step:rows + (j + 1) * step, :] = extra.astype(jnp.bfloat16)


def modes_kernel(mine_ref, other_ref, s_ref, y_ref, o_ref, e_ref, *, nf, nb, nm, nv, nx):
    nvx = nv * nx
    first = owned_half() == 0
    mine = mine_ref[...].astype(jnp.float32)
    other = other_ref[...].astype(jnp.float32)
    halves = (jnp.where(first, mine, other), jnp.where(first, other, mine))
    rows = mine.shape[0] // 2
    low = lax.broadcasted_iota(jnp.int32, (nm, 2 * nb), 1) < nb
    lane = lax.broadcasted_iota(jnp.int32, (nm, nf), 1)
    energy = jnp.zeros((nm, nf), jnp.float32)
    for f in range(nf):
        part = halves[f // (nf // 2)]
        at = (f % (nf // 2)) * nm
        coef = part[at:at + nm]
        extra = part[rows + at:rows + at + nm]
        energy = jnp.where(lane == f, extra[:, 0:1] + extra[:, 1:2] + extra[:, 2:3], energy)
        left = jnp.concatenate([jnp.where(low, coef, -coef), pltpu.roll(coef, nb, 1)], axis=0)
        m = jnp.dot(left.astype(jnp.bfloat16), y_ref[2 * nb * f:2 * nb * (f + 1), :],
                    preferred_element_type=jnp.float32)
        base = f * 2 * nm * nvx
        for c in range(nvx):
            v = c // nx
            o_ref[pl.ds(base + c, 2 * nm, stride=nvx), :] = (
                m[:, c * 128:(c + 1) * 128] * s_ref[v:v + 1, :])
    e_ref[...] = jnp.sqrt(energy / nb)


def shards(snapshots, quad_weight, mode_guess, bins, starts):
    nt, nv, nx, ny = snapshots.shape
    nf, nb, _, nm = mode_guess.shape
    nvx = nv * nx
    grid_points = nx * ny * lax.axis_size(SX) * lax.axis_size(SY)
    vmem = pl.BlockSpec(memory_space=pltpu.VMEM)
    hbm = pl.BlockSpec(memory_space=pltpu.HBM)
    params = pltpu.CompilerParams(vmem_limit_bytes=40 * MIB)

    x = snapshots.reshape(nt * nvx, ny)
    guess = jnp.transpose(mode_guess, (0, 2, 3, 1))
    nchunk = 4
    packed = nf // 2 * nv * nm + TAIL
    y, mine, other = pl.pallas_call(
        functools.partial(local_kernel, nf=nf, nb=nb, nt=nt, nm=nm, nv=nv, nx=nx),
        out_shape=(jax.ShapeDtypeStruct((nf * 2 * nb, nvx * ny), jnp.bfloat16),
                   jax.ShapeDtypeStruct((packed, 128), jnp.bfloat16),
                   jax.ShapeDtypeStruct((packed, 128), jnp.bfloat16)),
        in_specs=[hbm] * 5,
        out_specs=(vmem, vmem, vmem),
        scratch_shapes=[
            pltpu.VMEM((nchunk, nt * nvx // nchunk, ny), jnp.bfloat16),
            pltpu.VMEM((nt * nvx, ny), jnp.float32),
            pltpu.VMEM((nt, nvx * ny), jnp.bfloat16),
            pltpu.VMEM((nf * nv * nm, 128), jnp.bfloat16),
            pltpu.VMEM((nv, nx, ny), jnp.float32),
            pltpu.VMEM((nf, 2, nm, nb), jnp.float32),
            pltpu.VMEM((nb, 128), jnp.int32),
            pltpu.VMEM((nf + 8, 128), jnp.int32),
            pltpu.VMEM((2, nf + 8, nt), jnp.float32),
            pltpu.VMEM((2, nb, 128), jnp.float32),
            pltpu.VMEM((nb, nt), jnp.float32),
            pltpu.VMEM((2, 4 * nb, nt), jnp.bfloat16),
            pltpu.SMEM((nb,), jnp.int32),
            pltpu.SMEM((nf,), jnp.int32),
            pltpu.SemaphoreType.DMA((4 + nchunk,)),
        ],
        compiler_params=params,
        name="local_part",
    )(*[pltpu.with_memory_space_constraint(a, pltpu.HBM) for a in (starts, bins, x, quad_weight, guess)])
    swap = ((0, 1), (1, 0))
    received = [lax.ppermute(other, CORE, swap)]
    for step in STEPS + (LAST,):
        mine = pl.pallas_call(
            add_kernel,
            out_shape=jax.ShapeDtypeStruct((packed, 128), jnp.bfloat16),
            in_specs=[vmem] * (1 + len(received)), out_specs=vmem, compiler_params=params,
            name="add_partials",
        )(mine, *received)
        moves = [step] if len(step) == 1 else [step[:1], step[1:], step]
        received = [lax.ppermute(mine, AXES, flip_pairs(*move)) for move in moves]
    coef, scale = pl.pallas_call(
        functools.partial(owner_kernel, nv=nv, nm=nm, count=float(nt * grid_points),
                          denom=float(nv * grid_points)),
        out_shape=(jax.ShapeDtypeStruct((nf * nm, 128), jnp.bfloat16),
                   jax.ShapeDtypeStruct((8, 128), jnp.float32)),
        in_specs=[vmem, vmem], out_specs=(vmem, vmem), compiler_params=params, name="owner_part",
    )(mine, *received)
    coef_other = lax.ppermute(coef, CORE, swap)
    modes, energy = pl.pallas_call(
        functools.partial(modes_kernel, nf=nf, nb=nb, nm=nm, nv=nv, nx=nx),
        out_shape=(jax.ShapeDtypeStruct((nf * 2 * nm * nvx, ny), jnp.float32),
                   jax.ShapeDtypeStruct((nm, nf), jnp.float32)),
        in_specs=[vmem] * 4, out_specs=(vmem, vmem), compiler_params=params,
        name="modes_part",
    )(coef, coef_other, scale, y)
    return modes.reshape(nf, 2, nm, nv, nx, ny), energy.T


def solution(mesh):
    finer = Mesh(mesh.devices.reshape(SIZES), AXES)
    placed = (P(None, None, SX, SY), P(None, SX, SY), P(), P(), P())
    return jax.shard_map(
        shards,
        mesh=finer,
        in_specs=placed,
        out_specs=(P(None, None, None, None, SX, SY), P()),
        check_vma=False,
    )
```
